128 devices in a mesh: region: 32 (over z, x, core), obs: 4 (over y).
Axes of the slice: x: 4, y: 4, z: 4, core: 2. Of those that a mesh axis runs over, the one named last changes fastest.
Arguments:
- pattern: int32 [1048576], P(('region', 'obs')), may hold values from 0 to 511
- amplitude: float32 [5, 1048576], P(None, ('region', 'obs')), may hold values from 0.5 to 1.5
- basis_table: bfloat16 [5, 512, 128], replicated, may hold values from -2 to 2, as said below
- fields: bfloat16 [64, 1048576], P(None, ('region', 'obs')), may hold values from -24 to 24
- prior_precision: float32 [5, 128], replicated, may hold values from 16 to 512
Outputs:
- fitted: float32 [64, 1048576], P(None, ('region', 'obs'))
The draws below stay inside these ranges and needn't reach their ends.
Inputs may be any that keep to these rules, and one draw needn't show every extreme that they name: `basis_table`: basis rows of different tiers for one pattern are correlated.
All inputs are finite; a program needn't handle non-finite values.
Results may differ from the reference program's by a relative error of at most 0.0062.
Values sent between devices are 32-bit elements; how exact they have to be, the bound alone decides.
A program may use at most 64 MiB of HBM per device.

```python
import math
from functools import partial
import jax
import jax.numpy as jnp
from jax import lax

KNOTS = 128
FIELDS = 64
PATTERNS = 512
ANCESTORS = 4
TIERS = 5
LEAF_OBS = 32768
OBSERVATIONS = 1048576
N_REGION = 32


def draw_basis_table(key, part):
    shared_key, own_key = jax.random.split(jax.random.fold_in(key, 7))
    shared = jnp.clip(jax.random.normal(shared_key, (PATTERNS, KNOTS), jnp.float32), -4.0, 4.0)
    own = jnp.clip(jax.random.normal(own_key, (TIERS, PATTERNS, KNOTS), jnp.float32), -4.0, 4.0)
    mixed = (0.6 * shared[None] + 0.8 * own) * KNOTS ** (-0.5)
    return mixed.astype(jnp.bfloat16)


def touch_ends(result, stream_key, smallest, top_value):
    spot = [jax.random.randint(jax.random.fold_in(stream_key, axis), (), 0, length) for axis, length in enumerate(result.shape)]
    main_axis = result.shape.index(max(result.shape))
    beside = spot[:main_axis] + [(spot[main_axis] + 1) % result.shape[main_axis]] + spot[main_axis + 1:]
    return result.at[tuple(spot)].set(smallest).at[tuple(beside)].set(top_value)


def block_scale(rng, extent, cuts, smallest, largest):
    factor_of = 1.0
    for position, blocks in cuts:
        heights = jax.random.uniform(jax.random.fold_in(jax.random.fold_in(rng, 6), position), (blocks,), jnp.float32, smallest / len(cuts), largest / len(cuts))
        factor_of = factor_of * jnp.repeat(jnp.exp(heights), extent[position] // blocks).reshape((-1,) + (1,) * (len(extent) - 1 - position))
    return factor_of


def bell_draw(stream_key, dims, scale, most, cuts=(), dtype=jnp.bfloat16):
    factor_of = block_scale(stream_key, dims, cuts, -0.22, 0.18) if cuts else 1.0
    values = jax.random.normal(stream_key, dims, jnp.float32) * scale * factor_of
    return jnp.minimum(jnp.maximum(values, -most), most).astype(dtype)


def setup_inputs(seed: int = 0) -> dict:
    streams_of = jax.random.split(jax.random.key(seed), 6)
    return {
        "pattern": touch_ends(jax.random.randint(streams_of[0], (OBSERVATIONS,), 0, PATTERNS), jax.random.fold_in(streams_of[0], 1), 0, PATTERNS - 1).astype(jnp.int32),
        "amplitude": jnp.clip(0.5 + 1.0 * jax.random.uniform(streams_of[1], (TIERS, OBSERVATIONS), jnp.float32) ** block_scale(streams_of[1], (TIERS, OBSERVATIONS), ((1, 128),), -0.2, 0.2), 0.5, 1.5),
        "basis_table": draw_basis_table(jax.random.fold_in(streams_of[5], 71), 0),
        "fields": bell_draw(streams_of[3], (FIELDS, OBSERVATIONS), 4.0, 24.0, ((1, 128),)),
        "prior_precision": jnp.clip(jnp.exp(jax.random.uniform(streams_of[4], (TIERS, KNOTS), jnp.float32, math.log(16.0), math.log(512.0))), 16.0, 512.0),
    }


highest = lax.Precision.HIGHEST

def basis_rows(basis_table, pattern_rows, amplitude_rows):
    blocks = []
    for tier_index in range(basis_table.shape[0]):
        picked = jnp.take(basis_table[tier_index], pattern_rows, axis=0).astype(jnp.float32)
        blocks.append((picked * amplitude_rows[tier_index][:, None]).astype(jnp.bfloat16))
    return jnp.concatenate(blocks, axis=1)

def add_prior(matrix, prior_precision, tier_index):
    offset = tier_index * prior_precision.shape[1]
    return matrix.at[offset:, offset:].add(jnp.diag(prior_precision[tier_index]))

def eliminate(matrix, rhs_rows, tier_index, knot_count):
    offset = tier_index * knot_count
    factor = jnp.linalg.cholesky(matrix[offset:, offset:])
    whiten = lax.linalg.triangular_solve(factor, rhs_rows[:, offset:].T, left_side=True, lower=True)
    coupling = lax.linalg.triangular_solve(factor, matrix[offset:, :offset], left_side=True, lower=True)
    schur_part = matrix[:offset, :offset] - jnp.dot(coupling.T, coupling, precision=highest)
    reduced = rhs_rows[:, :offset] - jnp.dot(whiten.T, coupling, precision=highest)
    return (factor, coupling, whiten, schur_part, reduced)

def descend(factor, coupling, whiten, path):
    target = whiten - jnp.dot(coupling, path, precision=highest)
    return lax.linalg.triangular_solve(factor, target, left_side=True, lower=True, transpose_a=True)

def reference(pattern, amplitude, basis_table, fields, prior_precision):
    leaves = N_REGION
    pattern_leaf = pattern.reshape(leaves, LEAF_OBS)
    amplitude_leaf = amplitude.reshape(TIERS, leaves, LEAF_OBS).transpose(1, 0, 2)
    fields_leaf = fields.reshape(FIELDS, leaves, LEAF_OBS).transpose(1, 0, 2)

    def leaf_moments(inputs):
        pattern_rows, amplitude_rows, field_rows = inputs
        design = basis_rows(basis_table, pattern_rows, amplitude_rows)
        cross = lax.dot_general(design.astype(jnp.float32), design.astype(jnp.float32), (((0,), (0,)), ((), ())), preferred_element_type=jnp.float32)
        project = jnp.dot(field_rows.astype(jnp.float32), design.astype(jnp.float32), preferred_element_type=jnp.float32)
        return (cross, project)
    matrix, rhs_rows = lax.map(leaf_moments, (pattern_leaf, amplitude_leaf, fields_leaf))
    matrix = jax.vmap(partial(add_prior, prior_precision=prior_precision, tier_index=ANCESTORS))(matrix)
    stored = {}
    for tier_index in range(ANCESTORS, 0, -1):
        step_fn = partial(eliminate, tier_index=tier_index, knot_count=KNOTS)
        factor, coupling, whiten, schur_part, reduced = jax.vmap(step_fn)(matrix, rhs_rows)
        stored[tier_index] = (factor, coupling, whiten)
        if tier_index > 1:
            schur_part = schur_part.reshape((schur_part.shape[0] // 2, 2) + schur_part.shape[1:]).sum(axis=1)
            reduced = reduced.reshape((reduced.shape[0] // 2, 2) + reduced.shape[1:]).sum(axis=1)
        else:
            schur_part = schur_part.sum(axis=0, keepdims=True)
            reduced = reduced.sum(axis=0, keepdims=True)
        matrix = jax.vmap(partial(add_prior, prior_precision=prior_precision, tier_index=tier_index - 1))(schur_part)
        rhs_rows = reduced
    root_factor = jnp.linalg.cholesky(matrix[0])
    root_whiten = lax.linalg.triangular_solve(root_factor, rhs_rows[0].T, left_side=True, lower=True)
    root_weight = lax.linalg.triangular_solve(root_factor, root_whiten, left_side=True, lower=True, transpose_a=True)
    path = root_weight[None]
    for tier_index in range(1, TIERS):
        factor, coupling, whiten = stored[tier_index]
        parent_path = jnp.repeat(path, factor.shape[0] // path.shape[0], axis=0)
        local = jax.vmap(descend)(factor, coupling, whiten, parent_path)
        path = jnp.concatenate([parent_path, local], axis=1)
    path_weights = path.astype(jnp.bfloat16)

    def leaf_fitted(inputs):
        pattern_rows, amplitude_rows, weights = inputs
        design = basis_rows(basis_table, pattern_rows, amplitude_rows)
        return lax.dot_general(weights.astype(jnp.float32), design.astype(jnp.float32), (((0,), (1,)), ((), ())), preferred_element_type=jnp.float32)
    fitted_leaf = lax.map(leaf_fitted, (pattern_leaf, amplitude_leaf, path_weights))
    return fitted_leaf.transpose(1, 0, 2).reshape(FIELDS, leaves * LEAF_OBS)
```

```python
import functools

import jax
import jax.numpy as jnp
from jax import lax
from jax.experimental import pallas as pl
from jax.experimental.pallas import tpu as pltpu
from jax.sharding import PartitionSpec as P

f32 = jnp.float32
bf16 = jnp.bfloat16
highest = lax.Precision.HIGHEST
PANEL = 16
PAIR_ROW = {(0, 3): 5, (1, 4): 6, (0, 4): 7, (0, 1): 8, (1, 2): 9, (2, 3): 10, (3, 4): 11,
            (0, 2): 12, (1, 3): 13, (2, 4): 14, (0, 0): 0, (1, 1): 1, (2, 2): 2, (3, 3): 3, (4, 4): 4}


def iota(shape, axis):
    return lax.broadcasted_iota(jnp.int32, shape, axis)


def swapped(value, axis, stride):
    mask = 2**stride
    pairs = [(source, source ^ mask) for source in range(lax.axis_size(axis))]
    return lax.ppermute(value, axis, pairs)


def amplitude_products(amp):
    n = amp.shape[1]
    a8 = jnp.concatenate([amp, jnp.zeros((3, n), f32)], axis=0)
    sub = iota((8, n), 0)
    up = lambda s: pltpu.roll(a8, s, 0)
    l0 = jnp.where(sub < 5, a8, jnp.where(sub < 7, up(5), up(7)))
    r0 = jnp.where(sub < 5, a8, jnp.where(sub < 7, up(2), up(3)))
    l1 = jnp.where(sub < 4, a8, jnp.where(sub < 7, up(4), 0.0))
    r1 = jnp.where(sub < 4, up(7), up(2))
    return jnp.concatenate([l0 * r0, l1 * r1], axis=0)


def one_hot(pattern_ref, first_row, rows, patterns):
    parts = []
    ids = iota((patterns, 128), 0)
    for r in range(rows):
        row = pattern_ref[pl.ds(first_row + r, 1), :]
        parts.append((jnp.broadcast_to(row, (patterns, 128)) == ids).astype(f32).astype(bf16))
    return jnp.concatenate(parts, axis=1)


def stats_kernel(pattern_ref, amp_ref, table_ref, fields_ref, w_ref, c_ref, acc_ref, *, chunk):
    tiers, patterns, knots = table_ref.shape
    obs = amp_ref.shape[1]
    nf = fields_ref.shape[0]
    acc_ref[...] = jnp.zeros_like(acc_ref)

    def step(i, carry):
        off = pl.multiple_of(i * chunk, chunk)
        amp = amp_ref[:, pl.ds(off, chunk)]
        fields = fields_ref[:, pl.ds(off, chunk)].astype(f32)
        prod = amplitude_products(amp)
        hi = prod.astype(bf16)
        lo = (prod - hi.astype(f32)).astype(bf16)
        rows = [(fields * amp[t:t + 1, :]).astype(bf16) for t in range(tiers)]
        lhs = jnp.concatenate(rows + [hi, lo], axis=0)
        hot = one_hot(pattern_ref, i * (chunk // 128), chunk // 128, patterns)
        acc_ref[...] += lax.dot_general(lhs, hot, (((1,), (1,)), ((), ())), preferred_element_type=f32)
        return carry

    lax.fori_loop(0, obs // chunk, step, 0)
    base = tiers * nf
    w_ref[...] = acc_ref[base:base + 16, :] + acc_ref[base + 16:base + 32, :]
    for t in range(tiers):
        v = acc_ref[t * nf:(t + 1) * nf, :]
        hi = v.astype(bf16)
        lo = (v - hi.astype(f32)).astype(bf16)
        both = jnp.dot(jnp.concatenate([hi, lo], axis=0), table_ref[t], preferred_element_type=f32)
        c_ref[:, t * knots:(t + 1) * knots] = both[:nf] + both[nf:]


def fit_kernel(pattern_ref, amp_ref, f_ref, out_ref):
    tiers = amp_ref.shape[0]
    nf, chunk = out_ref.shape
    hot = one_hot(pattern_ref, 0, chunk // 128, f_ref.shape[1])
    part = jnp.dot(f_ref[...], hot, preferred_element_type=f32)
    total = part[:nf] * amp_ref[0:1, :]
    for t in range(1, tiers):
        total = total + part[t * nf:(t + 1) * nf] * amp_ref[t:t + 1, :]
    out_ref[...] = total


def inverse_factor_kernel(a_ref, o_ref, m_ref, q_ref):
    n = a_ref.shape[0]
    sub, lane, lane2 = iota((PANEL, n), 0), iota((PANEL, n), 1), iota((n, n), 1)
    m_ref[...] = a_ref[...]
    q_ref[...] = jnp.zeros((n, n), f32)

    def body(b, carry):
        off = pl.multiple_of(b * PANEL, PANEL)
        whole = m_ref[...]
        rows = m_ref[pl.ds(off, PANEL), :]
        cols = [
            jnp.take_along_axis(rows, jnp.zeros((PANEL, n), jnp.int32) + (off + l), axis=1)
            for l in range(PANEL)
        ]
        inside = (lane >= off) & (lane < off + PANEL)
        x = jnp.where(lane - off == sub, 1.0, jnp.where(inside, 0.0, rows))
        outs = x
        for j in range(PANEL):
            pick = lambda v: jnp.broadcast_to(v[j:j + 1, :], (PANEL, n))
            pivot = pick(cols[j])
            inv = 1.0 / pivot
            xj = pick(x)
            outs = jnp.where(sub == j, xj * lax.rsqrt(pivot), outs)
            mult = jnp.where(sub == j, inv, -cols[j] * inv)
            for l in range(j + 1, PANEL):
                cols[l] = jnp.where(sub == j, 0.0, cols[l]) + mult * pick(cols[l])
            x = jnp.where(sub == j, 0.0, x) + mult * xj
        o_ref[pl.ds(off, PANEL), :] = jnp.where(lane - off <= sub, outs, 0.0)
        q_ref[pl.ds(off, PANEL), :] = x
        update = jnp.dot(whole, q_ref[...], precision=highest, preferred_element_type=f32)
        q_ref[pl.ds(off, PANEL), :] = jnp.zeros((PANEL, n), f32)
        m_ref[...] = jnp.where((lane2 >= off) & (lane2 < off + PANEL), 0.0, whole) - update
        return carry

    lax.fori_loop(0, n // PANEL, body, 0)


def inverse_factor(a):
    n = a.shape[0]
    return pl.pallas_call(
        inverse_factor_kernel,
        out_shape=jax.ShapeDtypeStruct((n, n), f32),
        scratch_shapes=[pltpu.VMEM((n, n), f32)] * 2,
    )(a)


def add_prior(matrix, prior_precision, tier_index):
    offset = tier_index * prior_precision.shape[1]
    return matrix.at[offset:, offset:].add(jnp.diag(prior_precision[tier_index]))


def dot(a, b):
    return jnp.dot(a, b, precision=highest)


def eliminate(matrix, rhs_rows, tier_index, knot_count):
    offset = tier_index * knot_count
    factor = inverse_factor(matrix[offset:, offset:])
    whiten = dot(factor, rhs_rows[:, offset:].T)
    coupling = dot(factor, matrix[offset:, :offset])
    schur_part = matrix[:offset, :offset] - dot(coupling.T, coupling)
    reduced = rhs_rows[:, :offset] - dot(whiten.T, coupling)
    return (factor, coupling, whiten, schur_part, reduced)


def shards(pattern, amplitude, basis_table, fields, prior_precision):
    tiers, patterns, knots = basis_table.shape
    ancestors = tiers - 1
    obs = pattern.shape[0]
    nf = fields.shape[0]
    pattern2 = pattern.reshape(obs // 128, 128)
    w, c = pl.pallas_call(
        functools.partial(stats_kernel, chunk=1024),
        out_shape=(jax.ShapeDtypeStruct((16, patterns), f32), jax.ShapeDtypeStruct((nf, tiers * knots), f32)),
        scratch_shapes=[pltpu.VMEM((tiers * nf + 32, patterns), f32)],
    )(pattern2, amplitude, basis_table, fields)
    w, rhs_rows = lax.psum((w, c), "obs")
    table = basis_table.astype(f32)
    blocks = [[None] * tiers for _ in range(tiers)]
    for s in range(tiers):
        for t in range(s, tiers):
            blk = jnp.einsum("pk,pl->kl", table[t] * w[PAIR_ROW[(s, t)]][:, None], table[s], precision=highest)
            blocks[t][s] = blk
            blocks[s][t] = blk.T if t > s else blk
    matrix = jnp.concatenate([jnp.concatenate(row, axis=1) for row in blocks], axis=0)
    matrix = add_prior(matrix, prior_precision, ancestors)
    region_bits = lax.axis_size("region").bit_length() - 1
    stored = {}
    for tier_index in range(ancestors, 0, -1):
        factor, coupling, whiten, schur_part, reduced = eliminate(matrix, rhs_rows, tier_index, knots)
        stored[tier_index] = (factor, coupling, whiten)
        bits = [ancestors - tier_index] if tier_index > 1 else range(ancestors - 1, region_bits)
        for bit in bits:
            other_mat, other_rhs = swapped((schur_part, reduced), "region", bit)
            schur_part = schur_part + other_mat
            reduced = reduced + other_rhs
        matrix = add_prior(schur_part, prior_precision, tier_index - 1)
        rhs_rows = reduced
    root = inverse_factor(matrix)
    path = dot(root.T, dot(root, rhs_rows.T))
    for tier_index in range(1, tiers):
        factor, coupling, whiten = stored[tier_index]
        path = jnp.concatenate([path, dot(factor.T, whiten - dot(coupling, path))], axis=0)
    per_pattern = jnp.concatenate(
        [dot(path[t * knots:(t + 1) * knots].T, table[t].T) for t in range(tiers)], axis=0
    ).astype(bf16)
    chunk = min(1024, obs)
    return pl.pallas_call(
        fit_kernel,
        grid=(obs // chunk,),
        in_specs=[
            pl.BlockSpec((chunk // 128, 128), lambda i: (i, 0)),
            pl.BlockSpec((tiers, chunk), lambda i: (0, i)),
            pl.BlockSpec((tiers * nf, patterns), lambda i: (0, 0)),
        ],
        out_specs=pl.BlockSpec((nf, chunk), lambda i: (0, i)),
        out_shape=jax.ShapeDtypeStruct((nf, obs), f32),
    )(pattern2, amplitude, per_pattern)


def solution(mesh):
    return jax.shard_map(
        shards,
        mesh=mesh,
        in_specs=(
            P(("region", "obs")),
            P(None, ("region", "obs")),
            P(),
            P(None, ("region", "obs")),
            P(),
        ),
        out_specs=P(None, ("region", "obs")),
        check_vma=False,
    )
```

```python
import functools

import jax
import jax.numpy as jnp
from jax import lax
from jax.experimental import pallas as pl
from jax.experimental.pallas import tpu as pltpu
from jax.sharding import PartitionSpec as P

f32 = jnp.float32
bf16 = jnp.bfloat16
highest = lax.Precision.HIGHEST
PANEL = 16
PAIR_ROW = {(0, 3): 5, (1, 4): 6, (0, 4): 7, (0, 1): 8, (1, 2): 9, (2, 3): 10, (3, 4): 11,
            (0, 2): 12, (1, 3): 13, (2, 4): 14, (0, 0): 0, (1, 1): 1, (2, 2): 2, (3, 3): 3, (4, 4): 4}


def iota(shape, axis):
    return lax.broadcasted_iota(jnp.int32, shape, axis)


def amplitude_products(amp):
    n = amp.shape[1]
    a8 = jnp.concatenate([amp, jnp.zeros((3, n), f32)], axis=0)
    sub = iota((8, n), 0)
    up = lambda s: pltpu.roll(a8, s, 0)
    l0 = jnp.where(sub < 5, a8, jnp.where(sub < 7, up(5), up(7)))
    r0 = jnp.where(sub < 5, a8, jnp.where(sub < 7, up(2), up(3)))
    l1 = jnp.where(sub < 4, a8, jnp.where(sub < 7, up(4), 0.0))
    r1 = jnp.where(sub < 4, up(7), up(2))
    return jnp.concatenate([l0 * r0, l1 * r1], axis=0)


def one_hot(pattern_ref, first_row, rows, patterns):
    parts = []
    ids = iota((patterns, 128), 0)
    for r in range(rows):
        row = pattern_ref[pl.ds(first_row + r, 1), :]
        parts.append((jnp.broadcast_to(row, (patterns, 128)) == ids).astype(f32).astype(bf16))
    return jnp.concatenate(parts, axis=1)


def stats_kernel(pattern_ref, amp_ref, table_ref, fields_ref, w_ref, c_ref, acc_ref, *, chunk):
    tiers, patterns, knots = table_ref.shape
    obs = amp_ref.shape[1]
    nf = fields_ref.shape[0]
    acc_ref[...] = jnp.zeros_like(acc_ref)

    def step(i, carry):
        off = pl.multiple_of(i * chunk, chunk)
        amp = amp_ref[:, pl.ds(off, chunk)]
        fields = fields_ref[:, pl.ds(off, chunk)].astype(f32)
        prod = amplitude_products(amp)
        hi = prod.astype(bf16)
        lo = (prod - hi.astype(f32)).astype(bf16)
        rows = [(fields * amp[t:t + 1, :]).astype(bf16) for t in range(tiers)]
        lhs = jnp.concatenate(rows + [hi, lo], axis=0)
        hot = one_hot(pattern_ref, i * (chunk // 128), chunk // 128, patterns)
        acc_ref[...] += lax.dot_general(lhs, hot, (((1,), (1,)), ((), ())), preferred_element_type=f32)
        return carry

    lax.fori_loop(0, obs // chunk, step, 0)
    base = tiers * nf
    w_ref[...] = acc_ref[base:base + 16, :] + acc_ref[base + 16:base + 32, :]
    for t in range(tiers):
        v = acc_ref[t * nf:(t + 1) * nf, :]
        hi = v.astype(bf16)
        lo = (v - hi.astype(f32)).astype(bf16)
        both = jnp.dot(jnp.concatenate([hi, lo], axis=0), table_ref[t], preferred_element_type=f32)
        c_ref[t] = both[:nf] + both[nf:]


def fit_kernel(pattern_ref, amp_ref, f_ref, out_ref):
    tiers = amp_ref.shape[0]
    nf, chunk = out_ref.shape
    hot = one_hot(pattern_ref, 0, chunk // 128, f_ref.shape[1])
    part = jnp.dot(f_ref[...], hot, preferred_element_type=f32)
    total = part[:nf] * amp_ref[0:1, :]
    for t in range(1, tiers):
        total = total + part[t * nf:(t + 1) * nf] * amp_ref[t:t + 1, :]
    out_ref[...] = total


def inverse_factor(a, o_ref, m_ref, q_ref):
    n = a.shape[0]
    sub, lane, lane2 = iota((PANEL, n), 0), iota((PANEL, n), 1), iota((n, n), 1)
    m_ref[...] = a
    q_ref[...] = jnp.zeros((n, n), f32)

    def body(b, carry):
        off = pl.multiple_of(b * PANEL, PANEL)
        whole = m_ref[...]
        rows = m_ref[pl.ds(off, PANEL), :]
        cols = [
            jnp.take_along_axis(rows, jnp.zeros((PANEL, n), jnp.int32) + (off + l), axis=1)
            for l in range(PANEL)
        ]
        inside = (lane >= off) & (lane < off + PANEL)
        x = jnp.where(lane - off == sub, 1.0, jnp.where(inside, 0.0, rows))
        outs = x
        for j in range(PANEL):
            pick = lambda v: jnp.broadcast_to(v[j:j + 1, :], (PANEL, n))
            pivot = pick(cols[j])
            inv = 1.0 / pivot
            xj = pick(x)
            outs = jnp.where(sub == j, xj * lax.rsqrt(pivot), outs)
            mult = jnp.where(sub == j, inv, -cols[j] * inv)
            for l in range(j + 1, PANEL):
                cols[l] = jnp.where(sub == j, 0.0, cols[l]) + mult * pick(cols[l])
            x = jnp.where(sub == j, 0.0, x) + mult * xj
        o_ref[pl.ds(off, PANEL), :] = jnp.where(lane - off <= sub, outs, 0.0)
        q_ref[pl.ds(off, PANEL), :] = x
        update = jnp.dot(whole, q_ref[...], precision=highest, preferred_element_type=f32)
        q_ref[pl.ds(off, PANEL), :] = jnp.zeros((PANEL, n), f32)
        m_ref[...] = jnp.where((lane2 >= off) & (lane2 < off + PANEL), 0.0, whole) - update
        return carry

    lax.fori_loop(0, n // PANEL, body, 0)


def dot(a, b):
    return jnp.dot(a, b, precision=highest, preferred_element_type=f32)


def dot_nt(a, b):
    return lax.dot_general(a, b, (((1,), (1,)), ((), ())), precision=highest, preferred_element_type=f32)


def split2(v):
    hi = v.astype(bf16)
    return jnp.concatenate([hi, (v - hi.astype(f32)).astype(bf16)], axis=0)


def tri(t, s):
    return t * (t + 1) // 2 + s


def tree_kernel(wpart_ref, cpart_ref, table_ref, prior_ref, out_ref,
                bt_ref, wall_ref, cpiece_ref, csum_ref, g_ref, linv_ref, x_ref, z_ref, wt_ref, m_ref, q_ref,
                s4, s4r, c4, c4r, s3, s3r, c3, c3r, s2, s2r, c2, c2r, s1, s1r, c1, c1r, send_sem, recv_sem):
    tiers, patterns, knots = table_ref.shape
    nf = cpart_ref.shape[1]
    top = tiers - 1
    region, obs = lax.axis_index("region"), lax.axis_index("obs")
    n_obs = 4
    quarter = nf // n_obs
    own = {4: s4, 3: s3, 2: s2, 1: s1}
    got = {4: s4r, 3: s3r, 2: s2r, 1: s1r}
    cown = {4: c4, 3: c3, 2: c2, 1: c1}
    cgot = {4: c4r, 3: c3r, 2: c2r, 1: c1r}
    y_peers = [(region, lax.rem(obs + d, n_obs)) for d in range(1, n_obs)]

    def flip(*bits):
        other = region
        for bit in bits:
            other = other + bit - 2 * bit * lax.rem(lax.div(region, bit), 2)
        return other, obs

    tree_peer = {4: flip(1), 3: flip(2), 2: flip(2, 4)}
    z_peers = [flip(8), flip(8, 16), flip(16)]
    started = []

    def send(src, dst, k, dev):
        copy = pltpu.make_async_remote_copy(
            src_ref=src, dst_ref=dst, send_sem=send_sem.at[k], recv_sem=recv_sem.at[k],
            device_id=dev, device_id_type=pl.DeviceIdType.MESH)
        copy.start()
        started.append(copy)
        return copy

    barrier = pltpu.get_barrier_semaphore()
    peers = y_peers + list(tree_peer.values()) + z_peers
    for dev in peers:
        pl.semaphore_signal(barrier, inc=1, device_id=dev, device_id_type=pl.DeviceIdType.MESH)
    wall_ref[obs] = wpart_ref[...]
    pl.semaphore_wait(barrier, len(peers))

    w_copies = [send(wall_ref.at[obs], wall_ref.at[obs], k, dev) for k, dev in enumerate(y_peers)]
    rs_copies = [
        send(cpart_ref.at[:, pl.ds(pl.multiple_of(dev[1] * quarter, quarter), quarter), :], cpiece_ref.at[k], 3 + k, dev)
        for k, dev in enumerate(y_peers)
    ]
    for t in range(tiers):
        bt_ref[t] = table_ref[t].astype(f32).T.astype(bf16)
    for copy in w_copies:
        copy.wait_recv()
    w = (wall_ref[0] + wall_ref[1]) + (wall_ref[2] + wall_ref[3])
    for t in range(top, -1, -1):
        for s in range(t, -1, -1):
            row = PAIR_ROW[(s, t)]
            scaled = bt_ref[t].astype(f32) * w[row:row + 1, :]
            both = lax.dot_general(split2(scaled), bt_ref[s], (((1,), (1,)), ((), ())), preferred_element_type=f32)
            g_ref[tri(t, s)] = both[:knots] + both[knots:]
    for copy in rs_copies:
        copy.wait_recv()
    mine = pl.ds(pl.multiple_of(obs * quarter, quarter), quarter)
    csum_ref[:, mine, :] = cpart_ref[:, mine, :] + cpiece_ref[0] + cpiece_ref[1] + cpiece_ref[2]
    ag_copies = [
        send(csum_ref.at[:, mine, :], csum_ref.at[:, mine, :], 6 + k, dev) for k, dev in enumerate(y_peers)
    ]

    eye = iota((knots, knots), 0) == iota((knots, knots), 1)

    def factor(t, block):
        inverse_factor(block + jnp.where(eye, prior_ref[t:t + 1, :], 0.0), linv_ref.at[t], m_ref, q_ref)

    def eliminate(t, g, c, sem, before_rest, before_c):
        factor(t, g(t, t))
        linv = linv_ref[t]
        last = t - 1
        before_rest()
        xl = dot(linv, g(t, last))
        x_ref[tri(t - 1, last)] = xl
        own[t][tri(last, last)] = g(last, last) - dot(xl.T, xl)
        copies = []
        n_tri = tri(last, last)
        devs = z_peers if t == 1 else [tree_peer[t]]
        for k, dev in enumerate(devs):
            dst = got[t].at[k] if t == 1 else got[t].at[n_tri]
            copies.append(send(own[t].at[n_tri], dst, sem + k, dev))
        xs = [xl]
        if last:
            rest = dot(linv, jnp.concatenate([g(t, s) for s in range(last)], axis=1))
            xs = [rest[:, s * knots:(s + 1) * knots] for s in range(last)] + [xl]
            for s in range(last):
                x_ref[tri(t - 1, s)] = xs[s]
            for u in range(last, -1, -1):
                width = min(u + 1, last)
                prod = dot(xs[u].T, rest[:, :width * knots])
                for s in range(width):
                    own[t][tri(u, s)] = g(u, s) - prod[:, s * knots:(s + 1) * knots]
            for src, dst, k, dev in rest_parts(t, n_tri, sem):
                copies.append(send(src, dst, k, dev))
        before_c()
        z = dot_nt(c(t), linv)
        z_ref[t] = z
        red = dot(z, jnp.concatenate(xs, axis=1))
        for s in range(t):
            cown[t][s] = c(s) - red[:, s * knots:(s + 1) * knots]
        if t == 1:
            for k, dev in enumerate(devs):
                copies.append(send(cown[t].at[0], cgot[t].at[k], sem + 3 + k, dev))
        elif t == 3:
            part = pl.ds(pl.multiple_of(core * (nf // 2), nf // 2), nf // 2)
            copies.append(send(cown[t].at[:, part, :], cgot[t].at[:, part, :], sem + 2, devs[0]))
        else:
            copies.append(send(cown[t], cgot[t], sem + 2, devs[0]))
        return copies

    core = lax.rem(region, 2)
    half = pl.ds(pl.multiple_of(core * (knots // 2), knots // 2), knots // 2)

    def rest_parts(t, n_tri, sem):
        if t == 3:
            return [(own[t].at[pl.ds(0, n_tri), half, :], got[t].at[pl.ds(0, n_tri), half, :], sem + 1, tree_peer[t])]
        return [(own[t].at[pl.ds(0, n_tri)], got[t].at[pl.ds(0, n_tri)], sem + 1, tree_peer[t])]

    nothing = lambda: None

    def wait_ag():
        for copy in ag_copies:
            copy.wait_recv()

    e4 = eliminate(4, lambda t, s: g_ref[tri(t, s)], lambda s: csum_ref[s], 9, nothing, wait_ag)

    def summed(t):
        return lambda u, s: own[t][tri(u, s)] + got[t][tri(u, s)]

    def csummed(t):
        return lambda s: cown[t][s] + cgot[t][s]

    e4[0].wait_recv()
    e3 = eliminate(3, summed(4), csummed(4), 12, e4[1].wait_recv, e4[2].wait_recv)
    e3[0].wait_recv()
    relays = []

    def relay_rest():
        e3[1].wait_recv()
        part = got[3].at[pl.ds(0, 5), half, :]
        relays.append(send(part, part, 15, tree_peer[4]))
        e3[2].wait_recv()
        fields = pl.ds(pl.multiple_of(core * (nf // 2), nf // 2), nf // 2)
        part = cgot[3].at[:, fields, :]
        relays.append(send(part, part, 16, tree_peer[4]))
        relays[0].wait_recv()

    e2 = eliminate(2, summed(3), csummed(3), 17, relay_rest, lambda: relays[1].wait_recv())
    e2[0].wait_recv()
    e1 = eliminate(1, summed(2), csummed(2), 20, e2[1].wait_recv, e2[2].wait_recv)
    for copy in e1[:3]:
        copy.wait_recv()
    factor(0, (own[1][0] + got[1][0]) + (got[1][1] + got[1][2]))
    linv = linv_ref[0]
    for copy in e1[3:]:
        copy.wait_recv()
    c0 = (cown[1][0] + cgot[1][0]) + (cgot[1][1] + cgot[1][2])
    wts = [dot(dot_nt(c0, linv), linv)]
    for t in range(1, tiers):
        x = jnp.concatenate([x_ref[tri(t - 1, s)] for s in range(t)], axis=1)
        target = z_ref[t] - dot_nt(jnp.concatenate(wts, axis=1), x)
        wts.append(dot(target, linv_ref[t]))
    for t in range(tiers):
        both = jnp.dot(split2(wts[t]), bt_ref[t], preferred_element_type=f32)
        out_ref[t * nf:(t + 1) * nf, :] = (both[:nf] + both[nf:]).astype(bf16)
    for copy in started:
        copy.wait_send()


def shards(pattern, amplitude, basis_table, fields, prior_precision):
    tiers, patterns, knots = basis_table.shape
    obs = pattern.shape[0]
    nf = fields.shape[0]
    pattern2 = pattern.reshape(obs // 128, 128)
    w, c = pl.pallas_call(
        functools.partial(stats_kernel, chunk=1024),
        out_shape=(jax.ShapeDtypeStruct((16, patterns), f32), jax.ShapeDtypeStruct((tiers, nf, knots), f32)),
        scratch_shapes=[pltpu.VMEM((tiers * nf + 32, patterns), f32)],
    )(pattern2, amplitude, basis_table, fields)
    block = lambda n: pltpu.VMEM((n, knots, knots), f32)
    rhs = lambda n: pltpu.VMEM((n, nf, knots), f32)
    per_pattern = pl.pallas_call(
        tree_kernel,
        out_shape=jax.ShapeDtypeStruct((tiers * nf, patterns), bf16),
        scratch_shapes=[
            pltpu.VMEM((tiers, knots, patterns), bf16),
            pltpu.VMEM((4, 16, patterns), f32),
            pltpu.VMEM((3, tiers, nf // 4, knots), f32),
            rhs(tiers), block(15), block(5), block(10), rhs(5), rhs(5),
            pltpu.VMEM((knots, knots), f32), pltpu.VMEM((knots, knots), f32),
            block(10), block(10), rhs(4), rhs(4),
            block(6), block(6), rhs(3), rhs(3),
            block(3), block(3), rhs(2), rhs(2),
            block(1), block(3), rhs(1), rhs(3),
            pltpu.SemaphoreType.DMA((26,)), pltpu.SemaphoreType.DMA((26,)),
        ],
        compiler_params=pltpu.CompilerParams(collective_id=0, has_side_effects=True),
    )(w, c, basis_table, prior_precision)
    chunk = min(1024, obs)
    return pl.pallas_call(
        fit_kernel,
        grid=(obs // chunk,),
        in_specs=[
            pl.BlockSpec((chunk // 128, 128), lambda i: (i, 0)),
            pl.BlockSpec((tiers, chunk), lambda i: (0, i)),
            pl.BlockSpec((tiers * nf, patterns), lambda i: (0, 0)),
        ],
        out_specs=pl.BlockSpec((nf, chunk), lambda i: (0, i)),
        out_shape=jax.ShapeDtypeStruct((nf, obs), f32),
    )(pattern2, amplitude, per_pattern)


def solution(mesh):
    return jax.shard_map(
        shards,
        mesh=mesh,
        in_specs=(
            P(("region", "obs")),
            P(None, ("region", "obs")),
            P(),
            P(None, ("region", "obs")),
            P(),
        ),
        out_specs=P(None, ("region", "obs")),
        check_vma=False,
    )
```

```python
import functools

import jax
import jax.numpy as jnp
from jax import lax
from jax.experimental import pallas as pl
from jax.experimental.pallas import tpu as pltpu
from jax.sharding import PartitionSpec as P

f32 = jnp.float32
bf16 = jnp.bfloat16
highest = lax.Precision.HIGHEST
PANEL = 16
PAIR_ROW = {(0, 3): 5, (1, 4): 6, (0, 4): 7, (0, 1): 8, (1, 2): 9, (2, 3): 10, (3, 4): 11,
            (0, 2): 12, (1, 3): 13, (2, 4): 14, (0, 0): 0, (1, 1): 1, (2, 2): 2, (3, 3): 3, (4, 4): 4}


def iota(shape, axis):
    return lax.broadcasted_iota(jnp.int32, shape, axis)


def amplitude_products(amp):
    n = amp.shape[1]
    a8 = jnp.concatenate([amp, jnp.zeros((3, n), f32)], axis=0)
    sub = iota((8, n), 0)
    up = lambda s: pltpu.roll(a8, s, 0)
    l0 = jnp.where(sub < 5, a8, jnp.where(sub < 7, up(5), up(7)))
    r0 = jnp.where(sub < 5, a8, jnp.where(sub < 7, up(2), up(3)))
    l1 = jnp.where(sub < 4, a8, jnp.where(sub < 7, up(4), 0.0))
    r1 = jnp.where(sub < 4, up(7), up(2))
    return jnp.concatenate([l0 * r0, l1 * r1], axis=0)


def one_hot(pattern_ref, first_row, rows, patterns):
    parts = []
    ids = iota((patterns, 128), 0)
    for r in range(rows):
        row = pattern_ref[pl.ds(first_row + r, 1), :]
        parts.append((jnp.broadcast_to(row, (patterns, 128)) == ids).astype(f32).astype(bf16))
    return jnp.concatenate(parts, axis=1)


def accumulate(pattern_ref, amp_ref, fields_ref, acc_ref, chunk):
    tiers, obs = amp_ref.shape
    patterns = acc_ref.shape[1]
    acc_ref[...] = jnp.zeros_like(acc_ref)

    def step(i, carry):
        off = pl.multiple_of(i * chunk, chunk)
        amp = amp_ref[:, pl.ds(off, chunk)]
        fields = fields_ref[:, pl.ds(off, chunk)].astype(f32)
        prod = amplitude_products(amp)
        hi = prod.astype(bf16)
        lo = (prod - hi.astype(f32)).astype(bf16)
        rows = [(fields * amp[t:t + 1, :]).astype(bf16) for t in range(tiers)]
        lhs = jnp.concatenate(rows + [hi, lo], axis=0)
        hot = one_hot(pattern_ref, i * (chunk // 128), chunk // 128, patterns)
        acc_ref[...] += lax.dot_general(lhs, hot, (((1,), (1,)), ((), ())), preferred_element_type=f32)
        return carry

    lax.fori_loop(0, obs // chunk, step, 0)


def fit_kernel(pattern_ref, amp_ref, f_ref, out_ref):
    tiers = amp_ref.shape[0]
    nf, chunk = out_ref.shape
    hot = one_hot(pattern_ref, 0, chunk // 128, f_ref.shape[1])
    part = jnp.dot(f_ref[...], hot, preferred_element_type=f32)
    total = part[:nf] * amp_ref[0:1, :]
    for t in range(1, tiers):
        total = total + part[t * nf:(t + 1) * nf] * amp_ref[t:t + 1, :]
    out_ref[...] = total


def split3(v):
    hi = v.astype(bf16).astype(f32)
    rest = v - hi
    mid = rest.astype(bf16).astype(f32)
    return hi, mid, rest - mid


def inverse_factor(a, o_ref, m_ref, t_ref, tb_ref, q_ref):
    n = a.shape[0]
    sub, lane, lane2 = iota((PANEL, n), 0), iota((PANEL, n), 1), iota((n, n), 1)
    zero = jnp.zeros((PANEL, n), f32)
    m_ref[...] = a
    tb_ref[...] = jnp.zeros((n, n), bf16)
    q_ref[...] = jnp.zeros((n, n), bf16)

    def body(b, rows):
        off = pl.multiple_of(b * PANEL, PANEL)
        prev = off - PANEL
        cols = [
            jnp.take_along_axis(rows, jnp.zeros((PANEL, n), jnp.int32) + (off + l), axis=1)
            for l in range(PANEL)
        ]
        update = jnp.dot(tb_ref[...], q_ref[...], preferred_element_type=f32)
        hi, mid, low = split3(rows)
        turned = jnp.concatenate([rows, hi, hi, mid, hi, low, mid, zero], axis=0).T
        t_ref[...] = turned
        m_ref[...] = jnp.where((lane2 >= prev) & (lane2 < off), 0.0, m_ref[...]) - update
        tb_ref[...] = turned.astype(bf16)
        nxt = pl.multiple_of(jnp.minimum(off + PANEL, n - PANEL), PANEL)
        after = m_ref[pl.ds(nxt, PANEL), :]
        near = t_ref[pl.ds(nxt, PANEL), :]
        coup = [jnp.broadcast_to(near[:, l:l + 1], (PANEL, n)) for l in range(PANEL)]
        inside = (lane >= off) & (lane < off + PANEL)
        x = jnp.where(lane - off == sub, 1.0, jnp.where(inside, 0.0, rows))
        outs = invs = x
        for j in range(PANEL):
            pick = lambda v: jnp.broadcast_to(v[j:j + 1, :], (PANEL, n))
            inv = 1.0 / pick(cols[j])
            xj = pick(x)
            invs = jnp.where(sub == j, inv, invs)
            outs = jnp.where(sub == j, x, outs)
            mult = jnp.where(sub == j, 0.0, cols[j] * inv)
            for l in range(j + 1, PANEL):
                cols[l] = cols[l] - mult * pick(cols[l])
            x = x - mult * xj
        x = x * invs
        o_ref[pl.ds(off, PANEL), :] = jnp.where(lane - off <= sub, outs * jnp.sqrt(invs), 0.0)
        hi, mid, low = split3(x)
        q_ref[...] = jnp.concatenate([zero, hi, mid, hi, low, hi, mid, zero], axis=0).astype(bf16)
        terms = [coup[l] * jnp.broadcast_to(x[l:l + 1, :], (PANEL, n)) for l in range(PANEL)]
        while len(terms) > 1:
            terms = [terms[i] + terms[i + 1] for i in range(0, len(terms), 2)]
        return jnp.where(inside, 0.0, after) - terms[0]

    lax.fori_loop(0, n // PANEL, body, m_ref[0:PANEL, :])


def dot(a, b):
    return jnp.dot(a, b, precision=highest, preferred_element_type=f32)


def dot_nt(a, b):
    return lax.dot_general(a, b, (((1,), (1,)), ((), ())), precision=highest, preferred_element_type=f32)


def split2(v):
    hi = v.astype(bf16)
    return jnp.concatenate([hi, (v - hi.astype(f32)).astype(bf16)], axis=0)


def tri(t, s):
    return t * (t + 1) // 2 + s


def tree_kernel(pattern_ref, amp_ref, table_ref, fields_ref, prior_ref, out_ref,
                acc_ref, cpart_ref, bt_ref, wall_ref, cpiece_ref, csum_ref, g_ref, linv_ref, x_ref, z_ref, m_ref, t_ref, tb_ref, q_ref,
                s4, s4r, c4, c4r, s3, s3r, c3, c3r, s2, s2r, c2, c2r, s1, s1r, c1, c1r, send_sem, recv_sem):
    tiers, patterns, knots = table_ref.shape
    nf = fields_ref.shape[0]
    top = tiers - 1
    region, obs = lax.axis_index("region"), lax.axis_index("obs")
    n_obs = 4
    quarter = nf // n_obs
    own = {4: s4, 3: s3, 2: s2, 1: s1}
    got = {4: s4r, 3: s3r, 2: s2r, 1: s1r}
    cown = {4: c4, 3: c3, 2: c2, 1: c1}
    cgot = {4: c4r, 3: c3r, 2: c2r, 1: c1r}
    y_peers = [(region, lax.rem(obs + d, n_obs)) for d in range(1, n_obs)]

    def flip(*bits):
        other = region
        for bit in bits:
            other = other + bit - 2 * bit * lax.rem(lax.div(region, bit), 2)
        return other, obs

    tree_peer = {4: flip(1), 3: flip(2), 2: flip(2, 4)}
    z_peers = [flip(8), flip(8, 16), flip(16)]
    started = []

    def send(src, dst, k, dev):
        copy = pltpu.make_async_remote_copy(
            src_ref=src, dst_ref=dst, send_sem=send_sem.at[k], recv_sem=recv_sem.at[k],
            device_id=dev, device_id_type=pl.DeviceIdType.MESH)
        copy.start()
        started.append(copy)
        return copy

    barrier = pltpu.get_barrier_semaphore()
    peers = y_peers + list(tree_peer.values()) + z_peers
    for dev in peers:
        pl.semaphore_signal(barrier, inc=1, device_id=dev, device_id_type=pl.DeviceIdType.MESH)
    accumulate(pattern_ref, amp_ref, fields_ref, acc_ref, 1024)
    base = tiers * nf
    wall_ref[obs] = acc_ref[base:base + 16, :] + acc_ref[base + 16:base + 32, :]
    pl.semaphore_wait(barrier, len(peers))

    w_copies = [send(wall_ref.at[obs], wall_ref.at[obs], k, dev) for k, dev in enumerate(y_peers)]
    for t in range(tiers):
        v = split2(acc_ref[t * nf:(t + 1) * nf, :])
        both = jnp.dot(v, table_ref[t], preferred_element_type=f32)
        cpart_ref[t] = both[:nf] + both[nf:]
    rs_copies = [
        send(cpart_ref.at[:, pl.ds(pl.multiple_of(dev[1] * quarter, quarter), quarter), :], cpiece_ref.at[k], 3 + k, dev)
        for k, dev in enumerate(y_peers)
    ]
    for t in range(tiers):
        bt_ref[t] = table_ref[t].astype(f32).T.astype(bf16)
    for copy in w_copies:
        copy.wait_recv()
    w = (wall_ref[0] + wall_ref[1]) + (wall_ref[2] + wall_ref[3])
    for t in range(top, -1, -1):
        for s in range(t, -1, -1):
            row = PAIR_ROW[(s, t)]
            scaled = bt_ref[t].astype(f32) * w[row:row + 1, :]
            both = lax.dot_general(split2(scaled), bt_ref[s], (((1,), (1,)), ((), ())), preferred_element_type=f32)
            g_ref[tri(t, s)] = both[:knots] + both[knots:]
    for copy in rs_copies:
        copy.wait_recv()
    mine = pl.ds(pl.multiple_of(obs * quarter, quarter), quarter)
    csum_ref[:, mine, :] = cpart_ref[:, mine, :] + cpiece_ref[0] + cpiece_ref[1] + cpiece_ref[2]
    ag_copies = [
        send(csum_ref.at[:, mine, :], csum_ref.at[:, mine, :], 6 + k, dev) for k, dev in enumerate(y_peers)
    ]

    eye = iota((knots, knots), 0) == iota((knots, knots), 1)

    def factor(t, block):
        inverse_factor(block + jnp.where(eye, prior_ref[t:t + 1, :], 0.0), linv_ref.at[t], m_ref, t_ref, tb_ref, q_ref)

    def eliminate(t, g, c, sem, before_rest, before_c):
        factor(t, g(t, t))
        linv = linv_ref[t]
        last = t - 1
        before_rest()
        xl = dot(linv, g(t, last))
        x_ref[tri(t - 1, last)] = xl
        own[t][tri(last, last)] = g(last, last) - dot(xl.T, xl)
        copies = []
        n_tri = tri(last, last)
        devs = z_peers if t == 1 else [tree_peer[t]]
        for k, dev in enumerate(devs):
            dst = got[t].at[k] if t == 1 else got[t].at[n_tri]
            copies.append(send(own[t].at[n_tri], dst, sem + k, dev))
        xs = [xl]
        if last:
            rest = dot(linv, jnp.concatenate([g(t, s) for s in range(last)], axis=1))
            xs = [rest[:, s * knots:(s + 1) * knots] for s in range(last)] + [xl]
            for s in range(last):
                x_ref[tri(t - 1, s)] = xs[s]
            for u in range(last, -1, -1):
                width = min(u + 1, last)
                prod = dot(xs[u].T, rest[:, :width * knots])
                for s in range(width):
                    own[t][tri(u, s)] = g(u, s) - prod[:, s * knots:(s + 1) * knots]
            for src, dst, k, dev in rest_parts(t, n_tri, sem):
                copies.append(send(src, dst, k, dev))
        before_c()
        z = dot_nt(c(t), linv)
        z_ref[t] = z
        red = dot(z, jnp.concatenate(xs, axis=1))
        for s in range(t):
            cown[t][s] = c(s) - red[:, s * knots:(s + 1) * knots]
        if t == 1:
            for k, dev in enumerate(devs):
                copies.append(send(cown[t].at[0], cgot[t].at[k], sem + 3 + k, dev))
        elif t == 3:
            part = pl.ds(pl.multiple_of(core * (nf // 2), nf // 2), nf // 2)
            copies.append(send(cown[t].at[:, part, :], cgot[t].at[:, part, :], sem + 2, devs[0]))
        else:
            copies.append(send(cown[t], cgot[t], sem + 2, devs[0]))
        return copies

    core = lax.rem(region, 2)
    half = pl.ds(pl.multiple_of(core * (knots // 2), knots // 2), knots // 2)

    def rest_parts(t, n_tri, sem):
        if t == 3:
            return [(own[t].at[pl.ds(0, n_tri), half, :], got[t].at[pl.ds(0, n_tri), half, :], sem + 1, tree_peer[t])]
        return [(own[t].at[pl.ds(0, n_tri)], got[t].at[pl.ds(0, n_tri)], sem + 1, tree_peer[t])]

    nothing = lambda: None

    def wait_ag():
        for copy in ag_copies:
            copy.wait_recv()

    e4 = eliminate(4, lambda t, s: g_ref[tri(t, s)], lambda s: csum_ref[s], 9, nothing, wait_ag)

    def summed(t):
        return lambda u, s: own[t][tri(u, s)] + got[t][tri(u, s)]

    def csummed(t):
        return lambda s: cown[t][s] + cgot[t][s]

    e4[0].wait_recv()
    e3 = eliminate(3, summed(4), csummed(4), 12, e4[1].wait_recv, e4[2].wait_recv)
    e3[0].wait_recv()
    relays = []

    def relay_rest():
        e3[1].wait_recv()
        part = got[3].at[pl.ds(0, 5), half, :]
        relays.append(send(part, part, 15, tree_peer[4]))
        e3[2].wait_recv()
        fields = pl.ds(pl.multiple_of(core * (nf // 2), nf // 2), nf // 2)
        part = cgot[3].at[:, fields, :]
        relays.append(send(part, part, 16, tree_peer[4]))
        relays[0].wait_recv()

    e2 = eliminate(2, summed(3), csummed(3), 17, relay_rest, lambda: relays[1].wait_recv())
    e2[0].wait_recv()
    e1 = eliminate(1, summed(2), csummed(2), 20, e2[1].wait_recv, e2[2].wait_recv)
    for copy in e1[:3]:
        copy.wait_recv()
    factor(0, (own[1][0] + got[1][0]) + (got[1][1] + got[1][2]))
    linv = linv_ref[0]
    for copy in e1[3:]:
        copy.wait_recv()
    c0 = (cown[1][0] + cgot[1][0]) + (cgot[1][1] + cgot[1][2])
    wts = [dot(dot_nt(c0, linv), linv)]
    for t in range(1, tiers):
        x = jnp.concatenate([x_ref[tri(t - 1, s)] for s in range(t)], axis=1)
        target = z_ref[t] - dot_nt(jnp.concatenate(wts, axis=1), x)
        wts.append(dot(target, linv_ref[t]))
    for t in range(tiers):
        both = jnp.dot(split2(wts[t]), bt_ref[t], preferred_element_type=f32)
        out_ref[t * nf:(t + 1) * nf, :] = (both[:nf] + both[nf:]).astype(bf16)
    for copy in started:
        copy.wait_send()


def shards(pattern, amplitude, basis_table, fields, prior_precision):
    tiers, patterns, knots = basis_table.shape
    obs = pattern.shape[0]
    nf = fields.shape[0]
    pattern2 = pattern.reshape(obs // 128, 128)
    block = lambda n: pltpu.VMEM((n, knots, knots), f32)
    rhs = lambda n: pltpu.VMEM((n, nf, knots), f32)
    per_pattern = pl.pallas_call(
        tree_kernel,
        out_shape=jax.ShapeDtypeStruct((tiers * nf, patterns), bf16),
        scratch_shapes=[
            pltpu.VMEM((tiers * nf + 32, patterns), f32), rhs(tiers),
            pltpu.VMEM((tiers, knots, patterns), bf16),
            pltpu.VMEM((4, 16, patterns), f32),
            pltpu.VMEM((3, tiers, nf // 4, knots), f32),
            rhs(tiers), block(15), block(5), block(10), rhs(5),
            pltpu.VMEM((knots, knots), f32), pltpu.VMEM((knots, knots), f32),
            pltpu.VMEM((knots, knots), bf16), pltpu.VMEM((knots, knots), bf16),
            block(10), block(10), rhs(4), rhs(4),
            block(6), block(6), rhs(3), rhs(3),
            block(3), block(3), rhs(2), rhs(2),
            block(1), block(3), rhs(1), rhs(3),
            pltpu.SemaphoreType.DMA((26,)), pltpu.SemaphoreType.DMA((26,)),
        ],
        compiler_params=pltpu.CompilerParams(collective_id=0, has_side_effects=True),
    )(pattern2, amplitude, basis_table, fields, prior_precision)
    chunk = min(1024, obs)
    return pl.pallas_call(
        fit_kernel,
        grid=(obs // chunk,),
        in_specs=[
            pl.BlockSpec((chunk // 128, 128), lambda i: (i, 0)),
            pl.BlockSpec((tiers, chunk), lambda i: (0, i)),
            pl.BlockSpec((tiers * nf, patterns), lambda i: (0, 0)),
        ],
        out_specs=pl.BlockSpec((nf, chunk), lambda i: (0, i)),
        out_shape=jax.ShapeDtypeStruct((nf, obs), f32),
    )(pattern2, amplitude, per_pattern)


def solution(mesh):
    return jax.shard_map(
        shards,
        mesh=mesh,
        in_specs=(
            P(("region", "obs")),
            P(None, ("region", "obs")),
            P(),
            P(None, ("region", "obs")),
            P(),
        ),
        out_specs=P(None, ("region", "obs")),
        check_vma=False,
    )
```

```python
import functools

import jax
import jax.numpy as jnp
from jax import lax
from jax.experimental import pallas as pl
from jax.experimental.pallas import tpu as pltpu
from jax.sharding import PartitionSpec as P

f32 = jnp.float32
bf16 = jnp.bfloat16
highest = lax.Precision.HIGHEST
PANEL = 16
PAIR_ROW = {(0, 3): 5, (1, 4): 6, (0, 4): 7, (0, 1): 8, (1, 2): 9, (2, 3): 10, (3, 4): 11,
            (0, 2): 12, (1, 3): 13, (2, 4): 14, (0, 0): 0, (1, 1): 1, (2, 2): 2, (3, 3): 3, (4, 4): 4}


def iota(shape, axis):
    return lax.broadcasted_iota(jnp.int32, shape, axis)


def amplitude_products(amp):
    n = amp.shape[1]
    a8 = jnp.concatenate([amp, jnp.zeros((3, n), f32)], axis=0)
    sub = iota((8, n), 0)
    up = lambda s: pltpu.roll(a8, s, 0)
    l0 = jnp.where(sub < 5, a8, jnp.where(sub < 7, up(5), up(7)))
    r0 = jnp.where(sub < 5, a8, jnp.where(sub < 7, up(2), up(3)))
    l1 = jnp.where(sub < 4, a8, jnp.where(sub < 7, up(4), 0.0))
    r1 = jnp.where(sub < 4, up(7), up(2))
    return jnp.concatenate([l0 * r0, l1 * r1], axis=0)


def one_hot(pattern_ref, first_row, rows, patterns):
    parts = []
    ids = iota((patterns, 128), 0)
    for r in range(rows):
        row = pattern_ref[pl.ds(first_row + r, 1), :]
        parts.append((jnp.broadcast_to(row, (patterns, 128)) == ids).astype(f32).astype(bf16))
    return jnp.concatenate(parts, axis=1)


def accumulate(pattern_ref, amp_ref, fields_ref, acc_ref, chunk):
    tiers, obs = amp_ref.shape
    patterns = acc_ref.shape[1]
    acc_ref[...] = jnp.zeros_like(acc_ref)

    def step(i, carry):
        off = pl.multiple_of(i * chunk, chunk)
        amp = amp_ref[:, pl.ds(off, chunk)]
        fields = fields_ref[:, pl.ds(off, chunk)].astype(f32)
        prod = amplitude_products(amp)
        hi = prod.astype(bf16)
        lo = (prod - hi.astype(f32)).astype(bf16)
        rows = [(fields * amp[t:t + 1, :]).astype(bf16) for t in range(tiers)]
        lhs = jnp.concatenate(rows + [hi, lo], axis=0)
        hot = one_hot(pattern_ref, i * (chunk // 128), chunk // 128, patterns)
        acc_ref[...] += lax.dot_general(lhs, hot, (((1,), (1,)), ((), ())), preferred_element_type=f32)
        return carry

    lax.fori_loop(0, obs // chunk, step, 0)


def fit_kernel(pattern_ref, amp_ref, f_ref, out_ref):
    tiers = amp_ref.shape[0]
    nf, chunk = out_ref.shape
    hot = one_hot(pattern_ref, 0, chunk // 128, f_ref.shape[1])
    part = jnp.dot(f_ref[...], hot, preferred_element_type=f32)
    total = part[:nf] * amp_ref[0:1, :]
    for t in range(1, tiers):
        total = total + part[t * nf:(t + 1) * nf] * amp_ref[t:t + 1, :]
    out_ref[...] = total


def split3(v):
    hi = v.astype(bf16).astype(f32)
    rest = v - hi
    mid = rest.astype(bf16).astype(f32)
    return hi, mid, rest - mid


def inverse_factor(a, o_ref, m_ref, t_ref, tb_ref, q_ref, hook=None, hook_at=0):
    n = a.shape[0]
    sub, lane, lane2 = iota((PANEL, n), 0), iota((PANEL, n), 1), iota((n, n), 1)
    zero = jnp.zeros((PANEL, n), f32)
    m_ref[...] = a
    tb_ref[...] = jnp.zeros((n, n), bf16)
    q_ref[...] = jnp.zeros((n, n), bf16)

    def body(b, rows):
        if hook is not None:
            pl.when(b == hook_at)(hook)
        off = pl.multiple_of(b * PANEL, PANEL)
        prev = off - PANEL
        cols = [
            jnp.take_along_axis(rows, jnp.zeros((PANEL, n), jnp.int32) + (off + l), axis=1)
            for l in range(PANEL)
        ]
        update = jnp.dot(tb_ref[...], q_ref[...], preferred_element_type=f32)
        hi, mid, low = split3(rows)
        turned = jnp.concatenate([rows, hi, hi, mid, hi, low, mid, zero], axis=0).T
        t_ref[...] = turned
        m_ref[...] = jnp.where((lane2 >= prev) & (lane2 < off), 0.0, m_ref[...]) - update
        tb_ref[...] = turned.astype(bf16)
        nxt = pl.multiple_of(jnp.minimum(off + PANEL, n - PANEL), PANEL)
        after = m_ref[pl.ds(nxt, PANEL), :]
        near = t_ref[pl.ds(nxt, PANEL), :]
        coup = [jnp.broadcast_to(near[:, l:l + 1], (PANEL, n)) for l in range(PANEL)]
        inside = (lane >= off) & (lane < off + PANEL)
        x = jnp.where(lane - off == sub, 1.0, jnp.where(inside, 0.0, rows))
        outs = invs = x
        for j in range(PANEL):
            pick = lambda v: jnp.broadcast_to(v[j:j + 1, :], (PANEL, n))
            inv = 1.0 / pick(cols[j])
            xj = pick(x)
            invs = jnp.where(sub == j, inv, invs)
            outs = jnp.where(sub == j, x, outs)
            mult = jnp.where(sub == j, 0.0, cols[j] * inv)
            for l in range(j + 1, PANEL):
                cols[l] = cols[l] - mult * pick(cols[l])
            x = x - mult * xj
        x = x * invs
        o_ref[pl.ds(off, PANEL), :] = jnp.where(lane - off <= sub, outs * jnp.sqrt(invs), 0.0)
        hi, mid, low = split3(x)
        q_ref[...] = jnp.concatenate([zero, hi, mid, hi, low, hi, mid, zero], axis=0).astype(bf16)
        terms = [coup[l] * jnp.broadcast_to(x[l:l + 1, :], (PANEL, n)) for l in range(PANEL)]
        while len(terms) > 1:
            terms = [terms[i] + terms[i + 1] for i in range(0, len(terms), 2)]
        return jnp.where(inside, 0.0, after) - terms[0]

    lax.fori_loop(0, n // PANEL, body, m_ref[0:PANEL, :])


def pieces(v):
    hi = v.astype(bf16)
    rest = v - hi.astype(f32)
    mid = rest.astype(bf16)
    return hi, mid, (rest - mid.astype(f32)).astype(bf16)


def product(a, b, axis):
    ah, am, al = pieces(a)
    bh, bm, bl = pieces(b)
    left, right = jnp.concatenate([ah, am], axis=1), jnp.concatenate([ah, al], axis=1)
    deep = lambda u, v: jnp.concatenate([u, v], axis=axis)
    mul = lambda u, v: lax.dot_general(u, v, (((1,), (axis,)), ((), ())), preferred_element_type=f32)
    n = b.shape[1 - axis]
    small = mul(right, deep(bl, bh))
    if n == 128:
        both = mul(left, jnp.concatenate([deep(bh, bh), deep(bm, bm)], axis=1 - axis))
        return both[:, :n] + (both[:, n:] + small)
    return mul(left, deep(bh, bh)) + (mul(left, deep(bm, bm)) + small)


def dot(a, b):
    return product(a, b, 0)


def dot_nt(a, b):
    return product(a, b, 1)


def split2(v):
    hi = v.astype(bf16)
    return jnp.concatenate([hi, (v - hi.astype(f32)).astype(bf16)], axis=0)


def tri(t, s):
    return t * (t + 1) // 2 + s


def tree_kernel(pattern_ref, amp_ref, table_ref, fields_ref, prior_ref, out_ref,
                acc_ref, cpart_ref, bt_ref, wall_ref, cpiece_ref, csum_ref, g_ref, linv_ref, x_ref, xt_ref, yt_ref, z_ref, m_ref, t_ref, tb_ref, q_ref,
                s4, s4r, c4, c4r, s3, s3r, c3, c3r, s2, s2r, c2, c2r, s1, s1r, c1, c1r, send_sem, recv_sem):
    tiers, patterns, knots = table_ref.shape
    nf = fields_ref.shape[0]
    top = tiers - 1
    region, obs = lax.axis_index("region"), lax.axis_index("obs")
    n_obs = 4
    quarter = nf // n_obs
    own = {4: s4, 3: s3, 2: s2, 1: s1}
    got = {4: s4r, 3: s3r, 2: s2r, 1: s1r}
    cown = {4: c4, 3: c3, 2: c2, 1: c1}
    cgot = {4: c4r, 3: c3r, 2: c2r, 1: c1r}
    y_peers = [(region, lax.rem(obs + d, n_obs)) for d in range(1, n_obs)]

    def flip(*bits):
        other = region
        for bit in bits:
            other = other + bit - 2 * bit * lax.rem(lax.div(region, bit), 2)
        return other, obs

    tree_peer = {4: flip(1), 3: flip(2), 2: flip(2, 4)}
    z_peers = [flip(8), flip(8, 16), flip(16)]
    started = []

    def make(src, dst, k, dev):
        copy = pltpu.make_async_remote_copy(
            src_ref=src, dst_ref=dst, send_sem=send_sem.at[k], recv_sem=recv_sem.at[k],
            device_id=dev, device_id_type=pl.DeviceIdType.MESH)
        started.append(copy)
        return copy

    def send(src, dst, k, dev):
        copy = make(src, dst, k, dev)
        copy.start()
        return copy

    barrier = pltpu.get_barrier_semaphore()
    peers = y_peers + list(tree_peer.values()) + z_peers
    for dev in peers:
        pl.semaphore_signal(barrier, inc=1, device_id=dev, device_id_type=pl.DeviceIdType.MESH)
    accumulate(pattern_ref, amp_ref, fields_ref, acc_ref, 1024)
    base = tiers * nf
    wall_ref[obs] = acc_ref[base:base + 16, :] + acc_ref[base + 16:base + 32, :]
    pl.semaphore_wait(barrier, len(peers))

    w_copies = [send(wall_ref.at[obs], wall_ref.at[obs], k, dev) for k, dev in enumerate(y_peers)]
    for t in range(tiers):
        v = split2(acc_ref[t * nf:(t + 1) * nf, :])
        both = jnp.dot(v, table_ref[t], preferred_element_type=f32)
        cpart_ref[t] = both[:nf] + both[nf:]
    rs_copies = [
        send(cpart_ref.at[:, pl.ds(pl.multiple_of(dev[1] * quarter, quarter), quarter), :], cpiece_ref.at[k], 3 + k, dev)
        for k, dev in enumerate(y_peers)
    ]
    for t in range(tiers):
        bt_ref[t] = table_ref[t].astype(f32).T.astype(bf16)
    for copy in w_copies:
        copy.wait_recv()
    w = (wall_ref[0] + wall_ref[1]) + (wall_ref[2] + wall_ref[3])
    for t in range(top, -1, -1):
        for s in range(t, -1, -1):
            row = PAIR_ROW[(s, t)]
            scaled = bt_ref[t].astype(f32) * w[row:row + 1, :]
            both = lax.dot_general(split2(scaled), bt_ref[s], (((1,), (1,)), ((), ())), preferred_element_type=f32)
            g_ref[tri(t, s)] = both[:knots] + both[knots:]
    for copy in rs_copies:
        copy.wait_recv()
    mine = pl.ds(pl.multiple_of(obs * quarter, quarter), quarter)
    csum_ref[:, mine, :] = cpart_ref[:, mine, :] + cpiece_ref[0] + cpiece_ref[1] + cpiece_ref[2]
    ag_copies = [
        send(csum_ref.at[:, mine, :], csum_ref.at[:, mine, :], 6 + k, dev) for k, dev in enumerate(y_peers)
    ]

    eye = iota((knots, knots), 0) == iota((knots, knots), 1)
    core = lax.rem(region, 2)
    half = pl.ds(pl.multiple_of(core * (knots // 2), knots // 2), knots // 2)

    def factor(t, block, hook=None, hook_at=0):
        inverse_factor(block + jnp.where(eye, prior_ref[t:t + 1, :], 0.0), linv_ref.at[t],
                       m_ref, t_ref, tb_ref, q_ref, hook, hook_at)

    def first_block(t, g):
        last = t - 1
        xl = dot(linv_ref[t], g(t, last))
        x_ref[tri(last, last)] = xl
        xt_ref[tri(last, last)] = xl.T
        own[t][tri(last, last)] = g(last, last) - dot(xt_ref[tri(last, last)], xl)

    def other_blocks(t, g):
        last = t - 1
        rest = dot(linv_ref[t], jnp.concatenate([g(t, s) for s in range(last)], axis=1))
        for s in range(last):
            xs = rest[:, s * knots:(s + 1) * knots]
            x_ref[tri(last, s)] = xs
            xt_ref[tri(last, s)] = xs.T
        for u in range(last, -1, -1):
            width = min(u + 1, last)
            prod = dot(xt_ref[tri(last, u)], rest[:, :width * knots])
            for s in range(width):
                own[t][tri(u, s)] = g(u, s) - prod[:, s * knots:(s + 1) * knots]

    def projections(t, c):
        z = dot_nt(c(t), linv_ref[t])
        z_ref[t] = z
        red = dot(z, jnp.concatenate([x_ref[tri(t - 1, s)] for s in range(t)], axis=1))
        for s in range(t):
            cown[t][s] = c(s) - red[:, s * knots:(s + 1) * knots]

    def prepare_descent(t):
        y = dot(jnp.concatenate([xt_ref[tri(t - 1, s)] for s in range(t)], axis=0), linv_ref[t])
        for s in range(t):
            yt_ref[tri(t - 1, s)] = y[s * knots:(s + 1) * knots]
        z_ref[t] = dot(z_ref[t], linv_ref[t])

    def summed(t):
        return lambda u, s: own[t][tri(u, s)] + got[t][tri(u, s)]

    def csummed(t):
        return lambda s: cown[t][s] + cgot[t][s]

    g4 = lambda t, s: g_ref[tri(t, s)]
    sibling, across, beyond = tree_peer[4], tree_peer[3], tree_peer[2]

    factor(4, g4(4, 4))
    first_block(4, g4)
    a4 = send(s4.at[9], s4r.at[9], 9, sibling)
    other_blocks(4, g4)
    b4 = send(s4.at[pl.ds(0, 9)], s4r.at[pl.ds(0, 9)], 10, sibling)
    a4.wait_recv()

    g3 = summed(4)
    factor(3, g3(3, 3))
    b4.wait_recv()
    first_block(3, g3)
    a3 = send(s3.at[5], s3r.at[5], 12, across)
    other_blocks(3, g3)
    near, far = pl.ds(2, 3), pl.ds(0, 2)
    b3 = send(s3.at[near, half, :], s3r.at[near, half, :], 13, across)
    d3 = send(s3.at[far, half, :], s3r.at[far, half, :], 14, across)
    for copy in ag_copies:
        copy.wait_recv()
    projections(4, lambda s: csum_ref[s])
    e4 = send(c4, c4r, 11, sibling)
    a3.wait_recv()

    g2 = summed(3)
    relay_near = make(s3r.at[near, half, :], s3r.at[near, half, :], 16, sibling)

    def hand_over():
        b3.wait_recv()
        relay_near.start()

    factor(2, g2(2, 2), hand_over, 5)
    relay_near.wait_recv()
    first_block(2, g2)
    a2 = send(s2.at[2], s2r.at[2], 18, beyond)
    d3.wait_recv()
    relay_far = send(s3r.at[far, half, :], s3r.at[far, half, :], 17, sibling)
    e4.wait_recv()
    projections(3, csummed(4))
    e3 = send(c3, c3r, 15, across)
    relay_far.wait_recv()
    other_blocks(2, g2)
    b2 = send(s2.at[pl.ds(0, 2)], s2r.at[pl.ds(0, 2)], 19, beyond)
    a2.wait_recv()

    g1 = summed(2)
    factor(1, g1(1, 1))
    b2.wait_recv()
    first_block(1, g1)
    a1 = [send(s1.at[0], s1r.at[k], 21 + k, dev) for k, dev in enumerate(z_peers)]
    e3.wait_recv()
    projections(2, csummed(3))
    e2 = send(c2, c2r, 20, beyond)
    prepare_descent(4)
    prepare_descent(3)
    e2.wait_recv()
    projections(1, csummed(2))
    e1 = [send(c1.at[0], c1r.at[k], 24 + k, dev) for k, dev in enumerate(z_peers)]
    prepare_descent(2)
    prepare_descent(1)
    for copy in a1:
        copy.wait_recv()
    factor(0, (s1[0] + s1r[0]) + (s1r[1] + s1r[2]))
    for copy in e1:
        copy.wait_recv()
    c0 = (c1[0] + c1r[0]) + (c1r[1] + c1r[2])
    wts = [dot(dot_nt(c0, linv_ref[0]), linv_ref[0])]
    left = {t: z_ref[t] for t in range(1, tiers)}
    for s in range(top):
        moved = dot(wts[s], jnp.concatenate([yt_ref[tri(t - 1, s)] for t in range(s + 1, tiers)], axis=1))
        for t in range(s + 1, tiers):
            left[t] = left[t] - moved[:, (t - s - 1) * knots:(t - s) * knots]
        wts.append(left[s + 1])
    for t in range(tiers):
        both = jnp.dot(split2(wts[t]), bt_ref[t], preferred_element_type=f32)
        out_ref[t * nf:(t + 1) * nf, :] = (both[:nf] + both[nf:]).astype(bf16)
    for copy in started:
        copy.wait_send()


def shards(pattern, amplitude, basis_table, fields, prior_precision):
    tiers, patterns, knots = basis_table.shape
    obs = pattern.shape[0]
    nf = fields.shape[0]
    pattern2 = pattern.reshape(obs // 128, 128)
    block = lambda n: pltpu.VMEM((n, knots, knots), f32)
    rhs = lambda n: pltpu.VMEM((n, nf, knots), f32)
    per_pattern = pl.pallas_call(
        tree_kernel,
        out_shape=jax.ShapeDtypeStruct((tiers * nf, patterns), bf16),
        scratch_shapes=[
            pltpu.VMEM((tiers * nf + 32, patterns), f32), rhs(tiers),
            pltpu.VMEM((tiers, knots, patterns), bf16),
            pltpu.VMEM((4, 16, patterns), f32),
            pltpu.VMEM((3, tiers, nf // 4, knots), f32),
            rhs(tiers), block(15), block(5), block(10), block(10), block(10), rhs(5),
            pltpu.VMEM((knots, knots), f32), pltpu.VMEM((knots, knots), f32),
            pltpu.VMEM((knots, knots), bf16), pltpu.VMEM((knots, knots), bf16),
            block(10), block(10), rhs(4), rhs(4),
            block(6), block(6), rhs(3), rhs(3),
            block(3), block(3), rhs(2), rhs(2),
            block(1), block(3), rhs(1), rhs(3),
            pltpu.SemaphoreType.DMA((27,)), pltpu.SemaphoreType.DMA((27,)),
        ],
        compiler_params=pltpu.CompilerParams(collective_id=0, has_side_effects=True),
    )(pattern2, amplitude, basis_table, fields, prior_precision)
    chunk = min(1024, obs)
    return pl.pallas_call(
        fit_kernel,
        grid=(obs // chunk,),
        in_specs=[
            pl.BlockSpec((chunk // 128, 128), lambda i: (i, 0)),
            pl.BlockSpec((tiers, chunk), lambda i: (0, i)),
            pl.BlockSpec((tiers * nf, patterns), lambda i: (0, 0)),
        ],
        out_specs=pl.BlockSpec((nf, chunk), lambda i: (0, i)),
        out_shape=jax.ShapeDtypeStruct((nf, obs), f32),
    )(pattern2, amplitude, per_pattern)


def solution(mesh):
    return jax.shard_map(
        shards,
        mesh=mesh,
        in_specs=(
            P(("region", "obs")),
            P(None, ("region", "obs")),
            P(),
            P(None, ("region", "obs")),
            P(),
        ),
        out_specs=P(None, ("region", "obs")),
        check_vma=False,
    )
```

```python
import functools

import jax
import jax.numpy as jnp
from jax import lax
from jax.experimental import pallas as pl
from jax.experimental.pallas import tpu as pltpu
from jax.sharding import PartitionSpec as P

f32 = jnp.float32
bf16 = jnp.bfloat16
highest = lax.Precision.HIGHEST
PANEL = 16
PAIR_ROW = {(0, 3): 5, (1, 4): 6, (0, 4): 7, (0, 1): 8, (1, 2): 9, (2, 3): 10, (3, 4): 11,
            (0, 2): 12, (1, 3): 13, (2, 4): 14, (0, 0): 0, (1, 1): 1, (2, 2): 2, (3, 3): 3, (4, 4): 4}


def iota(shape, axis):
    return lax.broadcasted_iota(jnp.int32, shape, axis)


def amplitude_products(amp):
    n = amp.shape[1]
    a8 = jnp.concatenate([amp, jnp.zeros((3, n), f32)], axis=0)
    sub = iota((8, n), 0)
    up = lambda s: pltpu.roll(a8, s, 0)
    l0 = jnp.where(sub < 5, a8, jnp.where(sub < 7, up(5), up(7)))
    r0 = jnp.where(sub < 5, a8, jnp.where(sub < 7, up(2), up(3)))
    l1 = jnp.where(sub < 4, a8, jnp.where(sub < 7, up(4), 0.0))
    r1 = jnp.where(sub < 4, up(7), up(2))
    return jnp.concatenate([l0 * r0, l1 * r1], axis=0)


def one_hot(pattern_ref, first_row, rows, patterns):
    parts = []
    ids = iota((patterns, 128), 0)
    for r in range(rows):
        row = pattern_ref[pl.ds(first_row + r, 1), :]
        parts.append((jnp.broadcast_to(row, (patterns, 128)) == ids).astype(f32).astype(bf16))
    return jnp.concatenate(parts, axis=1)


def accumulate(pattern_ref, acc_ref, obs, chunk, lhs_of):
    patterns = acc_ref.shape[1]
    acc_ref[...] = jnp.zeros_like(acc_ref)

    def step(i, carry):
        lhs = lhs_of(pl.ds(pl.multiple_of(i * chunk, chunk), chunk))
        hot = one_hot(pattern_ref, i * (chunk // 128), chunk // 128, patterns)
        acc_ref[...] += lax.dot_general(lhs, hot, (((1,), (1,)), ((), ())), preferred_element_type=f32)
        return carry

    lax.fori_loop(0, obs // chunk, step, 0)


def fit_kernel(pattern_ref, amp_ref, f_ref, out_ref):
    tiers = amp_ref.shape[0]
    nf, chunk = out_ref.shape
    part_of = min(1024, chunk)
    for first in range(0, chunk, part_of):
        cut = slice(first, first + part_of)
        hot = one_hot(pattern_ref, first // 128, part_of // 128, f_ref.shape[1])
        part = jnp.dot(f_ref[...], hot, preferred_element_type=f32)
        total = part[:nf] * amp_ref[0:1, cut]
        for t in range(1, tiers):
            total = total + part[t * nf:(t + 1) * nf] * amp_ref[t:t + 1, cut]
        out_ref[:, cut] = total


def split3(v):
    hi = v.astype(bf16).astype(f32)
    rest = v - hi
    mid = rest.astype(bf16).astype(f32)
    return hi, mid, rest - mid


def inverse_factor(a, o_ref, m_ref, t_ref, tb_ref, q_ref, hook=None, hook_at=0):
    n = a.shape[0]
    sub, lane, lane2 = iota((PANEL, n), 0), iota((PANEL, n), 1), iota((n, n), 1)
    zero = jnp.zeros((PANEL, n), f32)
    m_ref[...] = a
    tb_ref[...] = jnp.zeros((n, n), bf16)
    q_ref[...] = jnp.zeros((n, n), bf16)

    def body(b, rows):
        if hook is not None:
            pl.when(b == hook_at)(hook)
        off = pl.multiple_of(b * PANEL, PANEL)
        prev = off - PANEL
        cols = [
            jnp.take_along_axis(rows, jnp.zeros((PANEL, n), jnp.int32) + (off + l), axis=1)
            for l in range(PANEL)
        ]
        update = jnp.dot(tb_ref[...], q_ref[...], preferred_element_type=f32)
        hi, mid, low = split3(rows)
        turned = jnp.concatenate([rows, hi, hi, mid, hi, low, mid, zero], axis=0).T
        t_ref[...] = turned
        m_ref[...] = jnp.where((lane2 >= prev) & (lane2 < off), 0.0, m_ref[...]) - update
        tb_ref[...] = turned.astype(bf16)
        nxt = pl.multiple_of(jnp.minimum(off + PANEL, n - PANEL), PANEL)
        after = m_ref[pl.ds(nxt, PANEL), :]
        near = t_ref[pl.ds(nxt, PANEL), :]
        coup = [jnp.broadcast_to(near[:, l:l + 1], (PANEL, n)) for l in range(PANEL)]
        inside = (lane >= off) & (lane < off + PANEL)
        x = jnp.where(lane - off == sub, 1.0, jnp.where(inside, 0.0, rows))
        outs = invs = x
        for j in range(PANEL):
            pick = lambda v: jnp.broadcast_to(v[j:j + 1, :], (PANEL, n))
            inv = 1.0 / pick(cols[j])
            xj = pick(x)
            invs = jnp.where(sub == j, inv, invs)
            outs = jnp.where(sub == j, x, outs)
            mult = jnp.where(sub == j, 0.0, cols[j] * inv)
            for l in range(j + 1, PANEL):
                cols[l] = cols[l] - mult * pick(cols[l])
            x = x - mult * xj
        x = x * invs
        o_ref[pl.ds(off, PANEL), :] = jnp.where(lane - off <= sub, outs * jnp.sqrt(invs), 0.0)
        hi, mid, low = split3(x)
        q_ref[...] = jnp.concatenate([zero, hi, mid, hi, low, hi, mid, zero], axis=0).astype(bf16)
        terms = [coup[l] * jnp.broadcast_to(x[l:l + 1, :], (PANEL, n)) for l in range(PANEL)]
        while len(terms) > 1:
            terms = [terms[i] + terms[i + 1] for i in range(0, len(terms), 2)]
        return jnp.where(inside, 0.0, after) - terms[0]

    lax.fori_loop(0, n // PANEL, body, m_ref[0:PANEL, :])


def pieces(v):
    hi = v.astype(bf16)
    rest = v - hi.astype(f32)
    mid = rest.astype(bf16)
    return hi, mid, (rest - mid.astype(f32)).astype(bf16)


def product(a, b, axis):
    ah, am, al = pieces(a)
    bh, bm, bl = pieces(b)
    left, right = jnp.concatenate([ah, am], axis=1), jnp.concatenate([ah, al], axis=1)
    deep = lambda u, v: jnp.concatenate([u, v], axis=axis)
    mul = lambda u, v: lax.dot_general(u, v, (((1,), (axis,)), ((), ())), preferred_element_type=f32)
    n = b.shape[1 - axis]
    small = mul(right, deep(bl, bh))
    if n == 128:
        both = mul(left, jnp.concatenate([deep(bh, bh), deep(bm, bm)], axis=1 - axis))
        return both[:, :n] + (both[:, n:] + small)
    return mul(left, deep(bh, bh)) + (mul(left, deep(bm, bm)) + small)


def dot(a, b):
    return product(a, b, 0)


def dot_nt(a, b):
    return product(a, b, 1)


def split2(v):
    hi = v.astype(bf16)
    return jnp.concatenate([hi, (v - hi.astype(f32)).astype(bf16)], axis=0)


def tri(t, s):
    return t * (t + 1) // 2 + s


def tree_kernel(pattern_ref, amp_ref, table_ref, fields_ref, prior_ref, out_ref,
                accw_ref, acc_ref, cpart_ref, bt_ref, wall_ref, cpiece_ref, csum_ref, g_ref, linv_ref, x_ref, xt_ref, yt_ref, z_ref, m_ref, t_ref, tb_ref, q_ref,
                s4, s4r, c4, c4r, s3, s3r, c3, c3r, s2, s2r, c2, c2r, s1, s1r, c1, c1r, root_ref, send_sem, recv_sem):
    tiers, patterns, knots = table_ref.shape
    nf = fields_ref.shape[0]
    top = tiers - 1
    region, obs = lax.axis_index("region"), lax.axis_index("obs")
    n_obs = 4
    quarter = nf // n_obs
    own = {4: s4, 3: s3, 2: s2, 1: s1}
    got = {4: s4r, 3: s3r, 2: s2r, 1: s1r}
    cown = {4: c4, 3: c3, 2: c2, 1: c1}
    cgot = {4: c4r, 3: c3r, 2: c2r, 1: c1r}
    y_peers = [(region, lax.rem(obs + d, n_obs)) for d in range(1, n_obs)]

    def flip(*bits):
        other = region
        for bit in bits:
            other = other + bit - 2 * bit * lax.rem(lax.div(region, bit), 2)
        return other, obs

    tree_peer = {4: flip(1), 3: flip(2), 2: flip(2, 4)}
    z_peers = [flip(8), flip(8, 16), flip(16)]
    started = []

    def make(src, dst, k, dev):
        copy = pltpu.make_async_remote_copy(
            src_ref=src, dst_ref=dst, send_sem=send_sem.at[k], recv_sem=recv_sem.at[k],
            device_id=dev, device_id_type=pl.DeviceIdType.MESH)
        started.append(copy)
        return copy

    def send(src, dst, k, dev):
        copy = make(src, dst, k, dev)
        copy.start()
        return copy

    barrier = pltpu.get_barrier_semaphore()
    peers = y_peers + list(tree_peer.values()) + z_peers
    for dev in peers:
        pl.semaphore_signal(barrier, inc=1, device_id=dev, device_id_type=pl.DeviceIdType.MESH)
    def amplitude_rows(cut):
        prod = amplitude_products(amp_ref[:, cut])
        hi = prod.astype(bf16)
        return jnp.concatenate([hi, (prod - hi.astype(f32)).astype(bf16)], axis=0)

    def field_rows(cut):
        amp = amp_ref[:, cut]
        fields = fields_ref[:, cut].astype(f32)
        return jnp.concatenate([(fields * amp[t:t + 1, :]).astype(bf16) for t in range(tiers)], axis=0)

    n_here = amp_ref.shape[1]
    accumulate(pattern_ref, accw_ref, n_here, 1024, amplitude_rows)
    wall_ref[obs] = accw_ref[0:16, :] + accw_ref[16:32, :]
    pl.semaphore_wait(barrier, len(peers))

    w_copies = [send(wall_ref.at[obs], wall_ref.at[obs], k, dev) for k, dev in enumerate(y_peers)]
    accumulate(pattern_ref, acc_ref, n_here, 1024, field_rows)
    for t in range(tiers):
        v = split2(acc_ref[t * nf:(t + 1) * nf, :])
        both = jnp.dot(v, table_ref[t], preferred_element_type=f32)
        cpart_ref[t] = both[:nf] + both[nf:]
    rs_copies = [
        send(cpart_ref.at[:, pl.ds(pl.multiple_of(dev[1] * quarter, quarter), quarter), :], cpiece_ref.at[k], 3 + k, dev)
        for k, dev in enumerate(y_peers)
    ]
    for t in range(tiers):
        bt_ref[t] = table_ref[t].astype(f32).T.astype(bf16)
    for copy in w_copies:
        copy.wait_recv()
    w = (wall_ref[0] + wall_ref[1]) + (wall_ref[2] + wall_ref[3])
    for t in range(top, -1, -1):
        for s in range(t, -1, -1):
            row = PAIR_ROW[(s, t)]
            scaled = bt_ref[t].astype(f32) * w[row:row + 1, :]
            both = lax.dot_general(split2(scaled), bt_ref[s], (((1,), (1,)), ((), ())), preferred_element_type=f32)
            g_ref[tri(t, s)] = both[:knots] + both[knots:]
    for copy in rs_copies:
        copy.wait_recv()
    mine = pl.ds(pl.multiple_of(obs * quarter, quarter), quarter)
    csum_ref[:, mine, :] = cpart_ref[:, mine, :] + cpiece_ref[0] + cpiece_ref[1] + cpiece_ref[2]
    ag_copies = [
        send(csum_ref.at[:, mine, :], csum_ref.at[:, mine, :], 6 + k, dev) for k, dev in enumerate(y_peers)
    ]

    eye = iota((knots, knots), 0) == iota((knots, knots), 1)
    core = lax.rem(region, 2)
    half = pl.ds(pl.multiple_of(core * (knots // 2), knots // 2), knots // 2)

    def factor(t, block, hook=None, hook_at=0):
        inverse_factor(block + jnp.where(eye, prior_ref[t:t + 1, :], 0.0), linv_ref.at[t],
                       m_ref, t_ref, tb_ref, q_ref, hook, hook_at)

    def first_block(t, g):
        last = t - 1
        xl = dot(linv_ref[t], g(t, last))
        x_ref[tri(last, last)] = xl
        xt_ref[tri(last, last)] = xl.T
        own[t][tri(last, last)] = g(last, last) - dot(xt_ref[tri(last, last)], xl)

    def other_blocks(t, g):
        last = t - 1
        rest = dot(linv_ref[t], jnp.concatenate([g(t, s) for s in range(last)], axis=1))
        for s in range(last):
            xs = rest[:, s * knots:(s + 1) * knots]
            x_ref[tri(last, s)] = xs
            xt_ref[tri(last, s)] = xs.T
        for u in range(last, -1, -1):
            width = min(u + 1, last)
            prod = dot(xt_ref[tri(last, u)], rest[:, :width * knots])
            for s in range(width):
                own[t][tri(u, s)] = g(u, s) - prod[:, s * knots:(s + 1) * knots]

    def projections(t, c):
        z = dot_nt(c(t), linv_ref[t])
        z_ref[t] = z
        red = dot(z, jnp.concatenate([x_ref[tri(t - 1, s)] for s in range(t)], axis=1))
        for s in range(t):
            cown[t][s] = c(s) - red[:, s * knots:(s + 1) * knots]

    def prepare_descent(t):
        y = dot(jnp.concatenate([xt_ref[tri(t - 1, s)] for s in range(t)], axis=0), linv_ref[t])
        for s in range(t):
            yt_ref[tri(t - 1, s)] = y[s * knots:(s + 1) * knots]
        z_ref[t] = dot(z_ref[t], linv_ref[t])

    def summed(t):
        return lambda u, s: own[t][tri(u, s)] + got[t][tri(u, s)]

    def csummed(t):
        return lambda s: cown[t][s] + cgot[t][s]

    g4 = lambda t, s: g_ref[tri(t, s)]
    sibling, across, beyond = tree_peer[4], tree_peer[3], tree_peer[2]

    factor(4, g4(4, 4))
    first_block(4, g4)
    a4 = send(s4.at[9], s4r.at[9], 9, sibling)
    other_blocks(4, g4)
    b4 = send(s4.at[pl.ds(0, 9)], s4r.at[pl.ds(0, 9)], 10, sibling)
    a4.wait_recv()

    g3 = summed(4)
    factor(3, g3(3, 3))
    b4.wait_recv()
    first_block(3, g3)
    a3 = send(s3.at[5], s3r.at[5], 12, across)
    other_blocks(3, g3)
    near, far = pl.ds(2, 3), pl.ds(0, 2)
    b3 = send(s3.at[near, half, :], s3r.at[near, half, :], 13, across)
    d3 = send(s3.at[far, half, :], s3r.at[far, half, :], 14, across)
    for copy in ag_copies:
        copy.wait_recv()
    projections(4, lambda s: csum_ref[s])
    e4 = send(c4, c4r, 11, sibling)
    a3.wait_recv()

    g2 = summed(3)
    relay_near = make(s3r.at[near, half, :], s3r.at[near, half, :], 16, sibling)

    def hand_over():
        b3.wait_recv()
        relay_near.start()

    factor(2, g2(2, 2), hand_over, 5)
    relay_near.wait_recv()
    first_block(2, g2)
    a2 = send(s2.at[2], s2r.at[2], 18, beyond)
    d3.wait_recv()
    relay_far = send(s3r.at[far, half, :], s3r.at[far, half, :], 17, sibling)
    e4.wait_recv()
    projections(3, csummed(4))
    e3 = send(c3, c3r, 15, across)
    relay_far.wait_recv()
    other_blocks(2, g2)
    b2 = send(s2.at[pl.ds(0, 2)], s2r.at[pl.ds(0, 2)], 19, beyond)
    a2.wait_recv()

    g1 = summed(2)
    factor(1, g1(1, 1))
    b2.wait_recv()
    first_block(1, g1)
    a1 = [send(s1.at[0, half, :], s1r.at[k, half, :], 21 + k, dev) for k, dev in enumerate(z_peers)]
    e3.wait_recv()
    projections(2, csummed(3))
    e2 = send(c2, c2r, 20, beyond)
    prepare_descent(4)
    prepare_descent(3)
    e2.wait_recv()
    projections(1, csummed(2))
    e1 = [send(c1.at[0], c1r.at[k], 24 + k, dev) for k, dev in enumerate(z_peers)]
    prepare_descent(2)
    prepare_descent(1)
    for copy in a1:
        copy.wait_recv()
    root_ref[half, :] = (s1[0, half, :] + s1r[0, half, :]) + (s1r[1, half, :] + s1r[2, half, :])
    whole = send(root_ref.at[half, :], root_ref.at[half, :], 27, sibling)
    whole.wait_recv()
    factor(0, root_ref[...])
    for copy in e1:
        copy.wait_recv()
    c0 = (c1[0] + c1r[0]) + (c1r[1] + c1r[2])
    wts = [dot(dot_nt(c0, linv_ref[0]), linv_ref[0])]
    left = {t: z_ref[t] for t in range(1, tiers)}
    for s in range(top):
        moved = dot(wts[s], jnp.concatenate([yt_ref[tri(t - 1, s)] for t in range(s + 1, tiers)], axis=1))
        for t in range(s + 1, tiers):
            left[t] = left[t] - moved[:, (t - s - 1) * knots:(t - s) * knots]
        wts.append(left[s + 1])
    for t in range(tiers):
        both = jnp.dot(split2(wts[t]), bt_ref[t], preferred_element_type=f32)
        out_ref[t * nf:(t + 1) * nf, :] = (both[:nf] + both[nf:]).astype(bf16)
    for copy in started:
        copy.wait_send()


def shards(pattern, amplitude, basis_table, fields, prior_precision):
    tiers, patterns, knots = basis_table.shape
    obs = pattern.shape[0]
    nf = fields.shape[0]
    pattern2 = pattern.reshape(obs // 128, 128)
    block = lambda n: pltpu.VMEM((n, knots, knots), f32)
    rhs = lambda n: pltpu.VMEM((n, nf, knots), f32)
    per_pattern = pl.pallas_call(
        tree_kernel,
        out_shape=jax.ShapeDtypeStruct((tiers * nf, patterns), bf16),
        scratch_shapes=[
            pltpu.VMEM((32, patterns), f32), pltpu.VMEM((tiers * nf, patterns), f32), rhs(tiers),
            pltpu.VMEM((tiers, knots, patterns), bf16),
            pltpu.VMEM((4, 16, patterns), f32),
            pltpu.VMEM((3, tiers, nf // 4, knots), f32),
            rhs(tiers), block(15), block(5), block(10), block(10), block(10), rhs(5),
            pltpu.VMEM((knots, knots), f32), pltpu.VMEM((knots, knots), f32),
            pltpu.VMEM((knots, knots), bf16), pltpu.VMEM((knots, knots), bf16),
            block(10), block(10), rhs(4), rhs(4),
            block(6), block(6), rhs(3), rhs(3),
            block(3), block(3), rhs(2), rhs(2),
            block(1), block(3), rhs(1), rhs(3), pltpu.VMEM((knots, knots), f32),
            pltpu.SemaphoreType.DMA((28,)), pltpu.SemaphoreType.DMA((28,)),
        ],
        compiler_params=pltpu.CompilerParams(collective_id=0, has_side_effects=True),
    )(pattern2, amplitude, basis_table, fields, prior_precision)
    chunk = min(2048, obs)
    return pl.pallas_call(
        fit_kernel,
        grid=(obs // chunk,),
        in_specs=[
            pl.BlockSpec((chunk // 128, 128), lambda i: (i, 0)),
            pl.BlockSpec((tiers, chunk), lambda i: (0, i)),
            pl.BlockSpec((tiers * nf, patterns), lambda i: (0, 0)),
        ],
        out_specs=pl.BlockSpec((nf, chunk), lambda i: (0, i)),
        out_shape=jax.ShapeDtypeStruct((nf, obs), f32),
    )(pattern2, amplitude, per_pattern)


def solution(mesh):
    return jax.shard_map(
        shards,
        mesh=mesh,
        in_specs=(
            P(("region", "obs")),
            P(None, ("region", "obs")),
            P(),
            P(None, ("region", "obs")),
            P(),
        ),
        out_specs=P(None, ("region", "obs")),
        check_vma=False,
    )
```

```python
import functools

import jax
import jax.numpy as jnp
from jax import lax
from jax.experimental import pallas as pl
from jax.experimental.pallas import tpu as pltpu
from jax.sharding import PartitionSpec as P

f32 = jnp.float32
bf16 = jnp.bfloat16
highest = lax.Precision.HIGHEST
PANEL = 16
PAIR_ROW = {(0, 3): 5, (1, 4): 6, (0, 4): 7, (0, 1): 8, (1, 2): 9, (2, 3): 10, (3, 4): 11,
            (0, 2): 12, (1, 3): 13, (2, 4): 14, (0, 0): 0, (1, 1): 1, (2, 2): 2, (3, 3): 3, (4, 4): 4}


def iota(shape, axis):
    return lax.broadcasted_iota(jnp.int32, shape, axis)


def amplitude_products(amp):
    n = amp.shape[1]
    a8 = jnp.concatenate([amp, jnp.zeros((3, n), f32)], axis=0)
    sub = iota((8, n), 0)
    up = lambda s: pltpu.roll(a8, s, 0)
    l0 = jnp.where(sub < 5, a8, jnp.where(sub < 7, up(5), up(7)))
    r0 = jnp.where(sub < 5, a8, jnp.where(sub < 7, up(2), up(3)))
    l1 = jnp.where(sub < 4, a8, jnp.where(sub < 7, up(4), 0.0))
    r1 = jnp.where(sub < 4, up(7), up(2))
    return jnp.concatenate([l0 * r0, l1 * r1], axis=0)


def one_hot(pattern_ref, first_row, rows, patterns, fold=None):
    parts, masks = [], []
    ids = iota((patterns, 128), 0)
    for r in range(rows):
        row = pattern_ref[pl.ds(first_row + r, 1), :]
        if fold is not None:
            below = row < fold
            masks.append(jnp.where(below, 1.0, 0.0))
            row = jnp.where(below, row, row - fold)
        parts.append((jnp.broadcast_to(row, (patterns, 128)) == ids).astype(f32).astype(bf16))
    hot = jnp.concatenate(parts, axis=1)
    return hot if fold is None else (hot, jnp.concatenate(masks, axis=1))


def accumulate(pattern_ref, acc_ref, obs, chunk, lhs_of, fold=None):
    patterns = acc_ref.shape[1]
    acc_ref[...] = jnp.zeros_like(acc_ref)

    def step(i, carry):
        lhs = lhs_of(pl.ds(pl.multiple_of(i * chunk, chunk), chunk))
        hot = one_hot(pattern_ref, i * (chunk // 128), chunk // 128, patterns, fold)
        if fold is not None:
            hot, below = hot
            first = lhs * below.astype(bf16)
            lhs = jnp.concatenate([first, lhs - first], axis=0)
        acc_ref[...] += lax.dot_general(lhs, hot, (((1,), (1,)), ((), ())), preferred_element_type=f32)
        return carry

    lax.fori_loop(0, obs // chunk, step, 0)


def fit_kernel(pattern_ref, amp_ref, f_ref, out_ref):
    tiers = amp_ref.shape[0]
    nf, chunk = out_ref.shape
    part_of = min(1024, chunk)
    for first in range(0, chunk, part_of):
        cut = slice(first, first + part_of)
        hot = one_hot(pattern_ref, first // 128, part_of // 128, f_ref.shape[1])
        part = jnp.dot(f_ref[...], hot, preferred_element_type=f32)
        total = part[:nf] * amp_ref[0:1, cut]
        for t in range(1, tiers):
            total = total + part[t * nf:(t + 1) * nf] * amp_ref[t:t + 1, cut]
        out_ref[:, cut] = total


def split3(v):
    hi = v.astype(bf16).astype(f32)
    rest = v - hi
    mid = rest.astype(bf16).astype(f32)
    return hi, mid, rest - mid


def inverse_factor(a, o_ref, m_ref, t_ref, tb_ref, q_ref, hook=None, hook_at=0):
    n = a.shape[0]
    sub, lane, lane2 = iota((PANEL, n), 0), iota((PANEL, n), 1), iota((n, n), 1)
    zero = jnp.zeros((PANEL, n), f32)
    m_ref[...] = a
    tb_ref[...] = jnp.zeros((n, n), bf16)
    q_ref[...] = jnp.zeros((n, n), bf16)

    def body(b, rows):
        if hook is not None:
            pl.when(b == hook_at)(hook)
        off = pl.multiple_of(b * PANEL, PANEL)
        prev = off - PANEL
        cols = [
            jnp.take_along_axis(rows, jnp.zeros((PANEL, n), jnp.int32) + (off + l), axis=1)
            for l in range(PANEL)
        ]
        update = jnp.dot(tb_ref[...], q_ref[...], preferred_element_type=f32)
        hi, mid, low = split3(rows)
        turned = jnp.concatenate([rows, hi, hi, mid, hi, low, mid, zero], axis=0).T
        t_ref[...] = turned
        m_ref[...] = jnp.where((lane2 >= prev) & (lane2 < off), 0.0, m_ref[...]) - update
        tb_ref[...] = turned.astype(bf16)
        nxt = pl.multiple_of(jnp.minimum(off + PANEL, n - PANEL), PANEL)
        after = m_ref[pl.ds(nxt, PANEL), :]
        near = t_ref[pl.ds(nxt, PANEL), :]
        coup = [jnp.broadcast_to(near[:, l:l + 1], (PANEL, n)) for l in range(PANEL)]
        inside = (lane >= off) & (lane < off + PANEL)
        x = jnp.where(lane - off == sub, 1.0, jnp.where(inside, 0.0, rows))
        outs = invs = x
        for j in range(PANEL):
            pick = lambda v: jnp.broadcast_to(v[j:j + 1, :], (PANEL, n))
            inv = 1.0 / pick(cols[j])
            xj = pick(x)
            invs = jnp.where(sub == j, inv, invs)
            outs = jnp.where(sub == j, x, outs)
            mult = jnp.where(sub == j, 0.0, cols[j] * inv)
            for l in range(j + 1, PANEL):
                cols[l] = cols[l] - mult * pick(cols[l])
            x = x - mult * xj
        x = x * invs
        o_ref[pl.ds(off, PANEL), :] = jnp.where(lane - off <= sub, outs * jnp.sqrt(invs), 0.0)
        hi, mid, low = split3(x)
        q_ref[...] = jnp.concatenate([zero, hi, mid, hi, low, hi, mid, zero], axis=0).astype(bf16)
        terms = [coup[l] * jnp.broadcast_to(x[l:l + 1, :], (PANEL, n)) for l in range(PANEL)]
        while len(terms) > 1:
            terms = [terms[i] + terms[i + 1] for i in range(0, len(terms), 2)]
        return jnp.where(inside, 0.0, after) - terms[0]

    lax.fori_loop(0, n // PANEL, body, m_ref[0:PANEL, :])


def pieces(v):
    hi = v.astype(bf16)
    rest = v - hi.astype(f32)
    mid = rest.astype(bf16)
    return hi, mid, (rest - mid.astype(f32)).astype(bf16)


def product(a, b, axis):
    ah, am, al = pieces(a)
    bh, bm, bl = pieces(b)
    left, right = jnp.concatenate([ah, am], axis=1), jnp.concatenate([ah, al], axis=1)
    deep = lambda u, v: jnp.concatenate([u, v], axis=axis)
    mul = lambda u, v: lax.dot_general(u, v, (((1,), (axis,)), ((), ())), preferred_element_type=f32)
    n = b.shape[1 - axis]
    small = mul(right, deep(bl, bh))
    if n == 128:
        both = mul(left, jnp.concatenate([deep(bh, bh), deep(bm, bm)], axis=1 - axis))
        return both[:, :n] + (both[:, n:] + small)
    return mul(left, deep(bh, bh)) + (mul(left, deep(bm, bm)) + small)


def dot(a, b):
    return product(a, b, 0)


def dot_nt(a, b):
    return product(a, b, 1)


def split2(v):
    hi = v.astype(bf16)
    return jnp.concatenate([hi, (v - hi.astype(f32)).astype(bf16)], axis=0)


def tri(t, s):
    return t * (t + 1) // 2 + s


def tree_kernel(pattern_ref, amp_ref, table_any, fields_any, prior_ref, out_ref,
                table_ref, fields_ref, load_sem, accw_ref, acc_ref, cpart_ref, bt_ref, wall_ref, cpiece_ref, csum_ref, g_ref, linv_ref, x_ref, xt_ref, yt_ref, z_ref, m_ref, t_ref, tb_ref, q_ref,
                s4, s4r, c4, c4r, s3, s3r, c3, c3r, s2, s2r, c2, c2r, s1, s1r, c1, c1r, send_sem, recv_sem):
    tiers, patterns, knots = table_ref.shape
    nf = fields_ref.shape[0]
    top = tiers - 1
    region, obs = lax.axis_index("region"), lax.axis_index("obs")
    n_obs = 4
    quarter = nf // n_obs
    own = {4: s4, 3: s3, 2: s2, 1: s1}
    got = {4: s4r, 3: s3r, 2: s2r, 1: s1r}
    cown = {4: c4, 3: c3, 2: c2, 1: c1}
    cgot = {4: c4r, 3: c3r, 2: c2r, 1: c1r}
    y_peers = [(region, lax.rem(obs + d, n_obs)) for d in range(1, n_obs)]

    def flip(*bits):
        other = region
        for bit in bits:
            other = other + bit - 2 * bit * lax.rem(lax.div(region, bit), 2)
        return other, obs

    tree_peer = {4: flip(1), 3: flip(2), 2: flip(2, 4)}
    z_peers = [flip(8), flip(8, 16), flip(16)]
    started = []

    def make(src, dst, k, dev):
        copy = pltpu.make_async_remote_copy(
            src_ref=src, dst_ref=dst, send_sem=send_sem.at[k], recv_sem=recv_sem.at[k],
            device_id=dev, device_id_type=pl.DeviceIdType.MESH)
        started.append(copy)
        return copy

    def send(src, dst, k, dev):
        copy = make(src, dst, k, dev)
        copy.start()
        return copy

    barrier = pltpu.get_barrier_semaphore()
    peers = y_peers + list(tree_peer.values()) + z_peers
    for dev in peers:
        pl.semaphore_signal(barrier, inc=1, device_id=dev, device_id_type=pl.DeviceIdType.MESH)
    loads = [pltpu.make_async_copy(fields_any, fields_ref, load_sem.at[0]),
             pltpu.make_async_copy(table_any, table_ref, load_sem.at[1])]
    for load in loads:
        load.start()

    def amplitude_rows(cut):
        prod = amplitude_products(amp_ref[:, cut])
        hi = prod.astype(bf16)
        return jnp.concatenate([hi, (prod - hi.astype(f32)).astype(bf16)], axis=0)

    def field_rows(cut):
        amp = amp_ref[:, cut]
        fields = fields_ref[:, cut].astype(f32)
        return jnp.concatenate([(fields * amp[t:t + 1, :]).astype(bf16) for t in range(tiers)], axis=0)

    n_here = amp_ref.shape[1]
    fold = patterns // 2
    accumulate(pattern_ref, accw_ref, n_here, 4096, amplitude_rows, fold)
    wall_ref[obs, :, 0:fold] = accw_ref[0:16, :] + accw_ref[16:32, :]
    wall_ref[obs, :, fold:patterns] = accw_ref[32:48, :] + accw_ref[48:64, :]
    pl.semaphore_wait(barrier, len(peers))

    w_copies = [send(wall_ref.at[obs], wall_ref.at[obs], k, dev) for k, dev in enumerate(y_peers)]
    for load in loads:
        load.wait()
    accumulate(pattern_ref, acc_ref, n_here, 2048, field_rows)
    for t in range(tiers):
        v = split2(acc_ref[t * nf:(t + 1) * nf, :])
        both = jnp.dot(v, table_ref[t], preferred_element_type=f32)
        cpart_ref[t] = both[:nf] + both[nf:]
    rs_copies = [
        send(cpart_ref.at[:, pl.ds(pl.multiple_of(dev[1] * quarter, quarter), quarter), :], cpiece_ref.at[k], 3 + k, dev)
        for k, dev in enumerate(y_peers)
    ]
    for t in range(tiers):
        bt_ref[t] = table_ref[t].astype(f32).T.astype(bf16)
    for copy in w_copies:
        copy.wait_recv()
    w = (wall_ref[0] + wall_ref[1]) + (wall_ref[2] + wall_ref[3])
    for t in range(top, -1, -1):
        for s in range(t, -1, -1):
            row = PAIR_ROW[(s, t)]
            scaled = bt_ref[t].astype(f32) * w[row:row + 1, :]
            both = lax.dot_general(split2(scaled), bt_ref[s], (((1,), (1,)), ((), ())), preferred_element_type=f32)
            g_ref[tri(t, s)] = both[:knots] + both[knots:]
    for copy in rs_copies:
        copy.wait_recv()
    mine = pl.ds(pl.multiple_of(obs * quarter, quarter), quarter)
    csum_ref[:, mine, :] = cpart_ref[:, mine, :] + cpiece_ref[0] + cpiece_ref[1] + cpiece_ref[2]
    ag_copies = [
        send(csum_ref.at[:, mine, :], csum_ref.at[:, mine, :], 6 + k, dev) for k, dev in enumerate(y_peers)
    ]

    eye = iota((knots, knots), 0) == iota((knots, knots), 1)
    core = lax.rem(region, 2)
    half = pl.ds(pl.multiple_of(core * (knots // 2), knots // 2), knots // 2)

    def factor(t, block, hook=None, hook_at=0):
        inverse_factor(block + jnp.where(eye, prior_ref[t:t + 1, :], 0.0), linv_ref.at[t],
                       m_ref, t_ref, tb_ref, q_ref, hook, hook_at)

    def first_block(t, g):
        last = t - 1
        xl = dot(linv_ref[t], g(t, last))
        x_ref[tri(last, last)] = xl
        xt_ref[tri(last, last)] = xl.T
        own[t][tri(last, last)] = g(last, last) - dot(xt_ref[tri(last, last)], xl)

    def other_blocks(t, g):
        last = t - 1
        rest = dot(linv_ref[t], jnp.concatenate([g(t, s) for s in range(last)], axis=1))
        for s in range(last):
            xs = rest[:, s * knots:(s + 1) * knots]
            x_ref[tri(last, s)] = xs
            xt_ref[tri(last, s)] = xs.T
        for u in range(last, -1, -1):
            width = min(u + 1, last)
            prod = dot(xt_ref[tri(last, u)], rest[:, :width * knots])
            for s in range(width):
                own[t][tri(u, s)] = g(u, s) - prod[:, s * knots:(s + 1) * knots]

    def projections(t, c):
        z = dot_nt(c(t), linv_ref[t])
        z_ref[t] = z
        red = dot(z, jnp.concatenate([x_ref[tri(t - 1, s)] for s in range(t)], axis=1))
        for s in range(t):
            cown[t][s] = c(s) - red[:, s * knots:(s + 1) * knots]

    def prepare_descent(t):
        y = dot(jnp.concatenate([xt_ref[tri(t - 1, s)] for s in range(t)], axis=0), linv_ref[t])
        for s in range(t):
            yt_ref[tri(t - 1, s)] = y[s * knots:(s + 1) * knots]
        z_ref[t] = dot(z_ref[t], linv_ref[t])

    def summed(t):
        return lambda u, s: own[t][tri(u, s)] + got[t][tri(u, s)]

    def csummed(t):
        return lambda s: cown[t][s] + cgot[t][s]

    g4 = lambda t, s: g_ref[tri(t, s)]
    sibling, across, beyond = tree_peer[4], tree_peer[3], tree_peer[2]

    factor(4, g4(4, 4))
    first_block(4, g4)
    a4 = send(s4.at[9], s4r.at[9], 9, sibling)
    other_blocks(4, g4)
    b4 = send(s4.at[pl.ds(0, 9)], s4r.at[pl.ds(0, 9)], 10, sibling)
    a4.wait_recv()

    g3 = summed(4)
    factor(3, g3(3, 3))
    b4.wait_recv()
    first_block(3, g3)
    a3 = send(s3.at[5], s3r.at[5], 12, across)
    other_blocks(3, g3)
    near, far = pl.ds(2, 3), pl.ds(0, 2)
    b3 = send(s3.at[near, half, :], s3r.at[near, half, :], 13, across)
    d3 = send(s3.at[far, half, :], s3r.at[far, half, :], 14, across)
    for copy in ag_copies:
        copy.wait_recv()
    projections(4, lambda s: csum_ref[s])
    e4 = send(c4, c4r, 11, sibling)
    a3.wait_recv()

    g2 = summed(3)
    relay_near = make(s3r.at[near, half, :], s3r.at[near, half, :], 16, sibling)

    def hand_over():
        b3.wait_recv()
        relay_near.start()

    factor(2, g2(2, 2), hand_over, 5)
    relay_near.wait_recv()
    first_block(2, g2)
    a2 = send(s2.at[2], s2r.at[2], 18, beyond)
    d3.wait_recv()
    relay_far = send(s3r.at[far, half, :], s3r.at[far, half, :], 17, sibling)
    e4.wait_recv()
    projections(3, csummed(4))
    e3 = send(c3, c3r, 15, across)
    relay_far.wait_recv()
    other_blocks(2, g2)
    b2 = send(s2.at[pl.ds(0, 2)], s2r.at[pl.ds(0, 2)], 19, beyond)
    a2.wait_recv()

    g1 = summed(2)
    factor(1, g1(1, 1))
    b2.wait_recv()
    first_block(1, g1)
    a1 = [send(s1.at[0], s1r.at[k], 21 + k, dev) for k, dev in enumerate(z_peers)]
    e3.wait_recv()
    projections(2, csummed(3))
    e2 = send(c2, c2r, 20, beyond)
    prepare_descent(4)
    prepare_descent(3)
    e2.wait_recv()
    projections(1, csummed(2))
    e1 = [send(c1.at[0], c1r.at[k], 24 + k, dev) for k, dev in enumerate(z_peers)]
    prepare_descent(2)
    prepare_descent(1)
    for copy in a1:
        copy.wait_recv()
    factor(0, (s1[0] + s1r[0]) + (s1r[1] + s1r[2]))
    for copy in e1:
        copy.wait_recv()
    c0 = (c1[0] + c1r[0]) + (c1r[1] + c1r[2])
    wts = [dot(dot_nt(c0, linv_ref[0]), linv_ref[0])]
    left = {t: z_ref[t] for t in range(1, tiers)}
    for s in range(top):
        moved = dot(wts[s], jnp.concatenate([yt_ref[tri(t - 1, s)] for t in range(s + 1, tiers)], axis=1))
        for t in range(s + 1, tiers):
            left[t] = left[t] - moved[:, (t - s - 1) * knots:(t - s) * knots]
        wts.append(left[s + 1])
    for t in range(tiers):
        both = jnp.dot(split2(wts[t]), bt_ref[t], preferred_element_type=f32)
        out_ref[t * nf:(t + 1) * nf, :] = (both[:nf] + both[nf:]).astype(bf16)
    for copy in started:
        copy.wait_send()


def shards(pattern, amplitude, basis_table, fields, prior_precision):
    tiers, patterns, knots = basis_table.shape
    obs = pattern.shape[0]
    nf = fields.shape[0]
    pattern2 = pattern.reshape(obs // 128, 128)
    block = lambda n: pltpu.VMEM((n, knots, knots), f32)
    rhs = lambda n: pltpu.VMEM((n, nf, knots), f32)
    per_pattern = pl.pallas_call(
        tree_kernel,
        out_shape=jax.ShapeDtypeStruct((tiers * nf, patterns), bf16),
        in_specs=[
            pl.BlockSpec(memory_space=pltpu.VMEM), pl.BlockSpec(memory_space=pltpu.VMEM),
            pl.BlockSpec(memory_space=pl.ANY), pl.BlockSpec(memory_space=pl.ANY),
            pl.BlockSpec(memory_space=pltpu.VMEM),
        ],
        scratch_shapes=[
            pltpu.VMEM(basis_table.shape, bf16), pltpu.VMEM(fields.shape, bf16), pltpu.SemaphoreType.DMA((2,)),
            pltpu.VMEM((64, patterns // 2), f32), pltpu.VMEM((tiers * nf, patterns), f32), rhs(tiers),
            pltpu.VMEM((tiers, knots, patterns), bf16),
            pltpu.VMEM((4, 16, patterns), f32),
            pltpu.VMEM((3, tiers, nf // 4, knots), f32),
            rhs(tiers), block(15), block(5), block(10), block(10), block(10), rhs(5),
            pltpu.VMEM((knots, knots), f32), pltpu.VMEM((knots, knots), f32),
            pltpu.VMEM((knots, knots), bf16), pltpu.VMEM((knots, knots), bf16),
            block(10), block(10), rhs(4), rhs(4),
            block(6), block(6), rhs(3), rhs(3),
            block(3), block(3), rhs(2), rhs(2),
            block(1), block(3), rhs(1), rhs(3),
            pltpu.SemaphoreType.DMA((27,)), pltpu.SemaphoreType.DMA((27,)),
        ],
        compiler_params=pltpu.CompilerParams(collective_id=0, has_side_effects=True),
    )(pattern2, amplitude, basis_table, fields, prior_precision)
    chunk = min(2048, obs)
    return pl.pallas_call(
        fit_kernel,
        grid=(obs // chunk,),
        in_specs=[
            pl.BlockSpec((chunk // 128, 128), lambda i: (i, 0)),
            pl.BlockSpec((tiers, chunk), lambda i: (0, i)),
            pl.BlockSpec((tiers * nf, patterns), lambda i: (0, 0)),
        ],
        out_specs=pl.BlockSpec((nf, chunk), lambda i: (0, i)),
        out_shape=jax.ShapeDtypeStruct((nf, obs), f32),
    )(pattern2, amplitude, per_pattern)


def solution(mesh):
    return jax.shard_map(
        shards,
        mesh=mesh,
        in_specs=(
            P(("region", "obs")),
            P(None, ("region", "obs")),
            P(),
            P(None, ("region", "obs")),
            P(),
        ),
        out_specs=P(None, ("region", "obs")),
        check_vma=False,
    )
```

```python
import functools

import jax
import jax.numpy as jnp
from jax import lax
from jax.experimental import pallas as pl
from jax.experimental.pallas import tpu as pltpu
from jax.sharding import PartitionSpec as P

f32 = jnp.float32
bf16 = jnp.bfloat16
highest = lax.Precision.HIGHEST
PANEL = 16
PAIR_ROW = {(0, 3): 5, (1, 4): 6, (0, 4): 7, (0, 1): 8, (1, 2): 9, (2, 3): 10, (3, 4): 11,
            (0, 2): 12, (1, 3): 13, (2, 4): 14, (0, 0): 0, (1, 1): 1, (2, 2): 2, (3, 3): 3, (4, 4): 4}


def iota(shape, axis):
    return lax.broadcasted_iota(jnp.int32, shape, axis)


def amplitude_products(amp):
    n = amp.shape[1]
    a8 = jnp.concatenate([amp, jnp.zeros((3, n), f32)], axis=0)
    sub = iota((8, n), 0)
    up = lambda s: pltpu.roll(a8, s, 0)
    l0 = jnp.where(sub < 5, a8, jnp.where(sub < 7, up(5), up(7)))
    r0 = jnp.where(sub < 5, a8, jnp.where(sub < 7, up(2), up(3)))
    l1 = jnp.where(sub < 4, a8, jnp.where(sub < 7, up(4), 0.0))
    r1 = jnp.where(sub < 4, up(7), up(2))
    return jnp.concatenate([l0 * r0, l1 * r1], axis=0)


def one_hot(pattern_ref, first_row, rows, patterns, fold=None):
    parts, masks = [], []
    ids = iota((patterns, 128), 0)
    for r in range(rows):
        row = pattern_ref[pl.ds(first_row + r, 1), :]
        if fold is not None:
            below = row < fold
            masks.append(jnp.where(below, 1.0, 0.0))
            row = jnp.where(below, row, row - fold)
        parts.append((jnp.broadcast_to(row, (patterns, 128)) == ids).astype(f32).astype(bf16))
    hot = jnp.concatenate(parts, axis=1)
    return hot if fold is None else (hot, jnp.concatenate(masks, axis=1))


def accumulate(pattern_ref, acc_ref, obs, chunk, lhs_of, fold=None):
    patterns = acc_ref.shape[1]
    acc_ref[...] = jnp.zeros_like(acc_ref)

    def step(i, carry):
        lhs = lhs_of(pl.ds(pl.multiple_of(i * chunk, chunk), chunk))
        hot = one_hot(pattern_ref, i * (chunk // 128), chunk // 128, patterns, fold)
        if fold is not None:
            hot, below = hot
            first = lhs * below.astype(bf16)
            lhs = jnp.concatenate([first, lhs - first], axis=0)
        acc_ref[...] += lax.dot_general(lhs, hot, (((1,), (1,)), ((), ())), preferred_element_type=f32)
        return carry

    lax.fori_loop(0, obs // chunk, step, 0)


def fit_kernel(pattern_ref, amp_ref, f_ref, out_ref):
    tiers = amp_ref.shape[0]
    nf, chunk = out_ref.shape
    part_of = min(1024, chunk)
    for first in range(0, chunk, part_of):
        cut = slice(first, first + part_of)
        hot = one_hot(pattern_ref, first // 128, part_of // 128, f_ref.shape[1])
        part = jnp.dot(f_ref[...], hot, preferred_element_type=f32)
        total = part[:nf] * amp_ref[0:1, cut]
        for t in range(1, tiers):
            total = total + part[t * nf:(t + 1) * nf] * amp_ref[t:t + 1, cut]
        out_ref[:, cut] = total


def split3(v):
    hi = v.astype(bf16).astype(f32)
    rest = v - hi
    mid = rest.astype(bf16).astype(f32)
    return hi, mid, rest - mid


def inverse_factor(a, o_ref, m_ref, t_ref, tb_ref, q_ref, hook=None, hook_at=0):
    n = a.shape[0]
    sub, lane, lane2 = iota((PANEL, n), 0), iota((PANEL, n), 1), iota((n, n), 1)
    zero = jnp.zeros((PANEL, n), f32)
    m_ref[...] = a
    tb_ref[...] = jnp.zeros((n, n), bf16)
    q_ref[...] = jnp.zeros((n, n), bf16)

    def body(b, rows):
        if hook is not None:
            pl.when(b == hook_at)(hook)
        off = pl.multiple_of(b * PANEL, PANEL)
        prev = off - PANEL
        cols = [
            jnp.take_along_axis(rows, jnp.zeros((PANEL, n), jnp.int32) + (off + l), axis=1)
            for l in range(PANEL)
        ]
        update = jnp.dot(tb_ref[...], q_ref[...], preferred_element_type=f32)
        hi, mid, low = split3(rows)
        turned = jnp.concatenate([rows, hi, hi, mid, hi, low, mid, zero], axis=0).T
        t_ref[...] = turned
        m_ref[...] = jnp.where((lane2 >= prev) & (lane2 < off), 0.0, m_ref[...]) - update
        tb_ref[...] = turned.astype(bf16)
        nxt = pl.multiple_of(jnp.minimum(off + PANEL, n - PANEL), PANEL)
        after = m_ref[pl.ds(nxt, PANEL), :]
        near = t_ref[pl.ds(nxt, PANEL), :]
        coup = [jnp.broadcast_to(near[:, l:l + 1], (PANEL, n)) for l in range(PANEL)]
        inside = (lane >= off) & (lane < off + PANEL)
        x = jnp.where(lane - off == sub, 1.0, jnp.where(inside, 0.0, rows))
        outs = invs = x
        for j in range(PANEL):
            pick = lambda v: jnp.broadcast_to(v[j:j + 1, :], (PANEL, n))
            inv = 1.0 / pick(cols[j])
            xj = pick(x)
            invs = jnp.where(sub == j, inv, invs)
            outs = jnp.where(sub == j, x, outs)
            mult = jnp.where(sub == j, 0.0, cols[j] * inv)
            for l in range(j + 1, PANEL):
                cols[l] = cols[l] - mult * pick(cols[l])
            x = x - mult * xj
        x = x * invs
        o_ref[pl.ds(off, PANEL), :] = jnp.where(lane - off <= sub, outs * jnp.sqrt(invs), 0.0)
        hi, mid, low = split3(x)
        q_ref[...] = jnp.concatenate([zero, hi, mid, hi, low, hi, mid, zero], axis=0).astype(bf16)
        terms = [coup[l] * jnp.broadcast_to(x[l:l + 1, :], (PANEL, n)) for l in range(PANEL)]
        while len(terms) > 1:
            terms = [terms[i] + terms[i + 1] for i in range(0, len(terms), 2)]
        return jnp.where(inside, 0.0, after) - terms[0]

    lax.fori_loop(0, n // PANEL, body, m_ref[0:PANEL, :])


def pieces(v):
    hi = v.astype(bf16)
    rest = v - hi.astype(f32)
    mid = rest.astype(bf16)
    return hi, mid, (rest - mid.astype(f32)).astype(bf16)


def product(a, b, axis):
    ah, am, al = pieces(a)
    bh, bm, bl = pieces(b)
    left, right = jnp.concatenate([ah, am], axis=1), jnp.concatenate([ah, al], axis=1)
    deep = lambda u, v: jnp.concatenate([u, v], axis=axis)
    mul = lambda u, v: lax.dot_general(u, v, (((1,), (axis,)), ((), ())), preferred_element_type=f32)
    n = b.shape[1 - axis]
    small = mul(right, deep(bl, bh))
    if n == 128:
        both = mul(left, jnp.concatenate([deep(bh, bh), deep(bm, bm)], axis=1 - axis))
        return both[:, :n] + (both[:, n:] + small)
    return mul(left, deep(bh, bh)) + (mul(left, deep(bm, bm)) + small)


def dot(a, b):
    return product(a, b, 0)


def dot_nt(a, b):
    return product(a, b, 1)


def split2(v):
    hi = v.astype(bf16)
    return jnp.concatenate([hi, (v - hi.astype(f32)).astype(bf16)], axis=0)


def tri(t, s):
    return t * (t + 1) // 2 + s


def tree_kernel(pattern_ref, amp_ref, table_any, fields_any, prior_ref, out_ref,
                table_ref, fields_ref, load_sem, accw_ref, acc_ref, cpart_ref, bt_ref, wall_ref, cpiece_ref, csum_ref, g_ref, linv_ref, x_ref, xt_ref, yt_ref, z_ref, m_ref, t_ref, tb_ref, q_ref,
                s4, s4r, c4, c4r, s3, s3r, c3, c3r, s2, s2r, c2, c2r, s1, s1r, c1, c1r, send_sem, recv_sem):
    tiers, patterns, knots = table_ref.shape
    nf = fields_ref.shape[0]
    top = tiers - 1
    region, obs = lax.axis_index("region"), lax.axis_index("obs")
    n_obs = 4
    quarter = nf // n_obs
    own = {4: s4, 3: s3, 2: s2, 1: s1}
    got = {4: s4r, 3: s3r, 2: s2r, 1: s1r}
    cown = {4: c4, 3: c3, 2: c2, 1: c1}
    cgot = {4: c4r, 3: c3r, 2: c2r, 1: c1r}
    y_peers = [(region, lax.rem(obs + d, n_obs)) for d in range(1, n_obs)]

    def flip(*bits):
        other = region
        for bit in bits:
            other = other + bit - 2 * bit * lax.rem(lax.div(region, bit), 2)
        return other, obs

    tree_peer = {4: flip(1), 3: flip(2), 2: flip(2, 4)}
    z_peers = [flip(8), flip(8, 16), flip(16)]
    started = []

    def make(src, dst, k, dev):
        copy = pltpu.make_async_remote_copy(
            src_ref=src, dst_ref=dst, send_sem=send_sem.at[k], recv_sem=recv_sem.at[k],
            device_id=dev, device_id_type=pl.DeviceIdType.MESH)
        started.append(copy)
        return copy

    def send(src, dst, k, dev):
        copy = make(src, dst, k, dev)
        copy.start()
        return copy

    barrier = pltpu.get_barrier_semaphore()
    peers = y_peers + list(tree_peer.values()) + z_peers
    for dev in peers:
        pl.semaphore_signal(barrier, inc=1, device_id=dev, device_id_type=pl.DeviceIdType.MESH)
    loads = [pltpu.make_async_copy(fields_any, fields_ref, load_sem.at[0]),
             pltpu.make_async_copy(table_any, table_ref, load_sem.at[1])]
    for load in loads:
        load.start()

    def amplitude_rows(cut):
        prod = amplitude_products(amp_ref[:, cut])
        hi = prod.astype(bf16)
        return jnp.concatenate([hi, (prod - hi.astype(f32)).astype(bf16)], axis=0)

    def field_rows(cut):
        amp = amp_ref[:, cut]
        fields = fields_ref[:, cut].astype(f32)
        return jnp.concatenate([(fields * amp[t:t + 1, :]).astype(bf16) for t in range(tiers)], axis=0)

    n_here = amp_ref.shape[1]
    fold = patterns // 2
    accumulate(pattern_ref, accw_ref, n_here, 4096, amplitude_rows, fold)
    wall_ref[obs, :, 0:fold] = accw_ref[0:16, :] + accw_ref[16:32, :]
    wall_ref[obs, :, fold:patterns] = accw_ref[32:48, :] + accw_ref[48:64, :]
    pl.semaphore_wait(barrier, len(peers))

    w_copies = [send(wall_ref.at[obs], wall_ref.at[obs], k, dev) for k, dev in enumerate(y_peers)]
    for load in loads:
        load.wait()
    accumulate(pattern_ref, acc_ref, n_here, 2048, field_rows)
    for t in range(tiers):
        v = split2(acc_ref[t * nf:(t + 1) * nf, :])
        both = jnp.dot(v, table_ref[t], preferred_element_type=f32)
        cpart_ref[t] = both[:nf] + both[nf:]
    rs_copies = [
        send(cpart_ref.at[:, pl.ds(pl.multiple_of(dev[1] * quarter, quarter), quarter), :], cpiece_ref.at[k], 3 + k, dev)
        for k, dev in enumerate(y_peers)
    ]
    for t in range(tiers):
        bt_ref[t] = table_ref[t].astype(f32).T.astype(bf16)
    for copy in w_copies:
        copy.wait_recv()
    w = (wall_ref[0] + wall_ref[1]) + (wall_ref[2] + wall_ref[3])

    def build(t, s):
        row = PAIR_ROW[(s, t)]
        scaled = bt_ref[t].astype(f32) * w[row:row + 1, :]
        both = lax.dot_general(split2(scaled), bt_ref[s], (((1,), (1,)), ((), ())), preferred_element_type=f32)
        g_ref[tri(t, s)] = both[:knots] + both[knots:]

    urgent = [(4, 4), (4, 3), (3, 3)]
    for t, s in urgent:
        build(t, s)
    eye = iota((knots, knots), 0) == iota((knots, knots), 1)
    core = lax.rem(region, 2)
    half = pl.ds(pl.multiple_of(core * (knots // 2), knots // 2), knots // 2)

    def factor(t, block, hook=None, hook_at=0):
        inverse_factor(block + jnp.where(eye, prior_ref[t:t + 1, :], 0.0), linv_ref.at[t],
                       m_ref, t_ref, tb_ref, q_ref, hook, hook_at)

    def first_block(t, g):
        last = t - 1
        xl = dot(linv_ref[t], g(t, last))
        x_ref[tri(last, last)] = xl
        xt_ref[tri(last, last)] = xl.T
        own[t][tri(last, last)] = g(last, last) - dot(xt_ref[tri(last, last)], xl)

    def other_blocks(t, g):
        last = t - 1
        rest = dot(linv_ref[t], jnp.concatenate([g(t, s) for s in range(last)], axis=1))
        for s in range(last):
            xs = rest[:, s * knots:(s + 1) * knots]
            x_ref[tri(last, s)] = xs
            xt_ref[tri(last, s)] = xs.T
        for u in range(last, -1, -1):
            width = min(u + 1, last)
            prod = dot(xt_ref[tri(last, u)], rest[:, :width * knots])
            for s in range(width):
                own[t][tri(u, s)] = g(u, s) - prod[:, s * knots:(s + 1) * knots]

    def projections(t, c):
        z = dot_nt(c(t), linv_ref[t])
        z_ref[t] = z
        red = dot(z, jnp.concatenate([x_ref[tri(t - 1, s)] for s in range(t)], axis=1))
        for s in range(t):
            cown[t][s] = c(s) - red[:, s * knots:(s + 1) * knots]

    def prepare_descent(t):
        y = dot(jnp.concatenate([xt_ref[tri(t - 1, s)] for s in range(t)], axis=0), linv_ref[t])
        for s in range(t):
            yt_ref[tri(t - 1, s)] = y[s * knots:(s + 1) * knots]
        z_ref[t] = dot(z_ref[t], linv_ref[t])

    def summed(t):
        return lambda u, s: own[t][tri(u, s)] + got[t][tri(u, s)]

    def csummed(t):
        return lambda s: cown[t][s] + cgot[t][s]

    g4 = lambda t, s: g_ref[tri(t, s)]
    sibling, across, beyond = tree_peer[4], tree_peer[3], tree_peer[2]

    factor(4, g4(4, 4))
    first_block(4, g4)
    a4 = send(s4.at[9], s4r.at[9], 9, sibling)
    for copy in rs_copies:
        copy.wait_recv()
    mine = pl.ds(pl.multiple_of(obs * quarter, quarter), quarter)
    csum_ref[:, mine, :] = cpart_ref[:, mine, :] + cpiece_ref[0] + cpiece_ref[1] + cpiece_ref[2]
    ag_copies = [
        send(csum_ref.at[:, mine, :], csum_ref.at[:, mine, :], 6 + k, dev) for k, dev in enumerate(y_peers)
    ]
    for t in range(top, -1, -1):
        for s in range(t, -1, -1):
            if (t, s) not in urgent:
                build(t, s)
    other_blocks(4, g4)
    b4 = send(s4.at[pl.ds(0, 9)], s4r.at[pl.ds(0, 9)], 10, sibling)
    a4.wait_recv()

    g3 = summed(4)
    factor(3, g3(3, 3))
    b4.wait_recv()
    first_block(3, g3)
    a3 = send(s3.at[5], s3r.at[5], 12, across)
    other_blocks(3, g3)
    near, far = pl.ds(2, 3), pl.ds(0, 2)
    b3 = send(s3.at[near, half, :], s3r.at[near, half, :], 13, across)
    d3 = send(s3.at[far, half, :], s3r.at[far, half, :], 14, across)
    for copy in ag_copies:
        copy.wait_recv()
    projections(4, lambda s: csum_ref[s])
    e4 = send(c4, c4r, 11, sibling)
    a3.wait_recv()

    g2 = summed(3)
    relay_near = make(s3r.at[near, half, :], s3r.at[near, half, :], 16, sibling)

    def hand_over():
        b3.wait_recv()
        relay_near.start()

    factor(2, g2(2, 2), hand_over, 5)
    relay_near.wait_recv()
    first_block(2, g2)
    a2 = send(s2.at[2], s2r.at[2], 18, beyond)
    d3.wait_recv()
    relay_far = send(s3r.at[far, half, :], s3r.at[far, half, :], 17, sibling)
    e4.wait_recv()
    projections(3, csummed(4))
    e3 = send(c3, c3r, 15, across)
    relay_far.wait_recv()
    other_blocks(2, g2)
    b2 = send(s2.at[pl.ds(0, 2)], s2r.at[pl.ds(0, 2)], 19, beyond)
    a2.wait_recv()

    g1 = summed(2)
    factor(1, g1(1, 1))
    b2.wait_recv()
    first_block(1, g1)
    a1 = [send(s1.at[0], s1r.at[k], 21 + k, dev) for k, dev in enumerate(z_peers)]
    e3.wait_recv()
    projections(2, csummed(3))
    e2 = send(c2, c2r, 20, beyond)
    prepare_descent(4)
    prepare_descent(3)
    e2.wait_recv()
    projections(1, csummed(2))
    e1 = [send(c1.at[0], c1r.at[k], 24 + k, dev) for k, dev in enumerate(z_peers)]
    prepare_descent(2)
    prepare_descent(1)
    for copy in a1:
        copy.wait_recv()
    factor(0, (s1[0] + s1r[0]) + (s1r[1] + s1r[2]))
    for copy in e1:
        copy.wait_recv()
    c0 = (c1[0] + c1r[0]) + (c1r[1] + c1r[2])
    wts = [dot(dot_nt(c0, linv_ref[0]), linv_ref[0])]
    left = {t: z_ref[t] for t in range(1, tiers)}
    for s in range(top):
        moved = dot(wts[s], jnp.concatenate([yt_ref[tri(t - 1, s)] for t in range(s + 1, tiers)], axis=1))
        for t in range(s + 1, tiers):
            left[t] = left[t] - moved[:, (t - s - 1) * knots:(t - s) * knots]
        wts.append(left[s + 1])
    for t in range(tiers):
        both = jnp.dot(split2(wts[t]), bt_ref[t], preferred_element_type=f32)
        out_ref[t * nf:(t + 1) * nf, :] = (both[:nf] + both[nf:]).astype(bf16)
    for copy in started:
        copy.wait_send()


def shards(pattern, amplitude, basis_table, fields, prior_precision):
    tiers, patterns, knots = basis_table.shape
    obs = pattern.shape[0]
    nf = fields.shape[0]
    pattern2 = pattern.reshape(obs // 128, 128)
    block = lambda n: pltpu.VMEM((n, knots, knots), f32)
    rhs = lambda n: pltpu.VMEM((n, nf, knots), f32)
    per_pattern = pl.pallas_call(
        tree_kernel,
        out_shape=jax.ShapeDtypeStruct((tiers * nf, patterns), bf16),
        in_specs=[
            pl.BlockSpec(memory_space=pltpu.VMEM), pl.BlockSpec(memory_space=pltpu.VMEM),
            pl.BlockSpec(memory_space=pl.ANY), pl.BlockSpec(memory_space=pl.ANY),
            pl.BlockSpec(memory_space=pltpu.VMEM),
        ],
        scratch_shapes=[
            pltpu.VMEM(basis_table.shape, bf16), pltpu.VMEM(fields.shape, bf16), pltpu.SemaphoreType.DMA((2,)),
            pltpu.VMEM((64, patterns // 2), f32), pltpu.VMEM((tiers * nf, patterns), f32), rhs(tiers),
            pltpu.VMEM((tiers, knots, patterns), bf16),
            pltpu.VMEM((4, 16, patterns), f32),
            pltpu.VMEM((3, tiers, nf // 4, knots), f32),
            rhs(tiers), block(15), block(5), block(10), block(10), block(10), rhs(5),
            pltpu.VMEM((knots, knots), f32), pltpu.VMEM((knots, knots), f32),
            pltpu.VMEM((knots, knots), bf16), pltpu.VMEM((knots, knots), bf16),
            block(10), block(10), rhs(4), rhs(4),
            block(6), block(6), rhs(3), rhs(3),
            block(3), block(3), rhs(2), rhs(2),
            block(1), block(3), rhs(1), rhs(3),
            pltpu.SemaphoreType.DMA((27,)), pltpu.SemaphoreType.DMA((27,)),
        ],
        compiler_params=pltpu.CompilerParams(collective_id=0, has_side_effects=True),
    )(pattern2, amplitude, basis_table, fields, prior_precision)
    chunk = min(2048, obs)
    return pl.pallas_call(
        fit_kernel,
        grid=(obs // chunk,),
        in_specs=[
            pl.BlockSpec((chunk // 128, 128), lambda i: (i, 0)),
            pl.BlockSpec((tiers, chunk), lambda i: (0, i)),
            pl.BlockSpec((tiers * nf, patterns), lambda i: (0, 0)),
        ],
        out_specs=pl.BlockSpec((nf, chunk), lambda i: (0, i)),
        out_shape=jax.ShapeDtypeStruct((nf, obs), f32),
    )(pattern2, amplitude, per_pattern)


def solution(mesh):
    return jax.shard_map(
        shards,
        mesh=mesh,
        in_specs=(
            P(("region", "obs")),
            P(None, ("region", "obs")),
            P(),
            P(None, ("region", "obs")),
            P(),
        ),
        out_specs=P(None, ("region", "obs")),
        check_vma=False,
    )
```

```python
import functools

import jax
import jax.numpy as jnp
from jax import lax
from jax.experimental import pallas as pl
from jax.experimental.pallas import tpu as pltpu
from jax.sharding import PartitionSpec as P

f32 = jnp.float32
bf16 = jnp.bfloat16
highest = lax.Precision.HIGHEST
PANEL = 16
PAIR_ROW = {(0, 3): 5, (1, 4): 6, (0, 4): 7, (0, 1): 8, (1, 2): 9, (2, 3): 10, (3, 4): 11,
            (0, 2): 12, (1, 3): 13, (2, 4): 14, (0, 0): 0, (1, 1): 1, (2, 2): 2, (3, 3): 3, (4, 4): 4}


def iota(shape, axis):
    return lax.broadcasted_iota(jnp.int32, shape, axis)


def amplitude_products(amp):
    n = amp.shape[1]
    a8 = jnp.concatenate([amp, jnp.zeros((3, n), f32)], axis=0)
    sub = iota((8, n), 0)
    up = lambda s: pltpu.roll(a8, s, 0)
    l0 = jnp.where(sub < 5, a8, jnp.where(sub < 7, up(5), up(7)))
    r0 = jnp.where(sub < 5, a8, jnp.where(sub < 7, up(2), up(3)))
    l1 = jnp.where(sub < 4, a8, jnp.where(sub < 7, up(4), 0.0))
    r1 = jnp.where(sub < 4, up(7), up(2))
    return jnp.concatenate([l0 * r0, l1 * r1], axis=0)


def one_hot(pattern_ref, first_row, rows, patterns, fold=None):
    parts, masks = [], []
    ids = iota((patterns, 128), 0)
    for r in range(rows):
        row = pattern_ref[pl.ds(first_row + r, 1), :]
        if fold is not None:
            below = row < fold
            masks.append(jnp.where(below, 1.0, 0.0))
            row = jnp.where(below, row, row - fold)
        parts.append((jnp.broadcast_to(row, (patterns, 128)) == ids).astype(f32).astype(bf16))
    hot = jnp.concatenate(parts, axis=1)
    return hot if fold is None else (hot, jnp.concatenate(masks, axis=1))


def accumulate(pattern_ref, acc_ref, obs, chunk, lhs_of, fold=None):
    patterns = acc_ref.shape[1]
    acc_ref[...] = jnp.zeros_like(acc_ref)

    def step(i, carry):
        lhs = lhs_of(pl.ds(pl.multiple_of(i * chunk, chunk), chunk))
        hot = one_hot(pattern_ref, i * (chunk // 128), chunk // 128, patterns, fold)
        if fold is not None:
            hot, below = hot
            first = lhs * below.astype(bf16)
            lhs = jnp.concatenate([first, lhs - first], axis=0)
        acc_ref[...] += lax.dot_general(lhs, hot, (((1,), (1,)), ((), ())), preferred_element_type=f32)
        return carry

    lax.fori_loop(0, obs // chunk, step, 0)


def fit_kernel(pattern_ref, amp_ref, f_ref, out_ref):
    tiers = amp_ref.shape[0]
    nf, chunk = out_ref.shape
    part_of = min(1024, chunk)
    for first in range(0, chunk, part_of):
        cut = slice(first, first + part_of)
        hot = one_hot(pattern_ref, first // 128, part_of // 128, f_ref.shape[1])
        part = jnp.dot(f_ref[...], hot, preferred_element_type=f32)
        total = part[:nf] * amp_ref[0:1, cut]
        for t in range(1, tiers):
            total = total + part[t * nf:(t + 1) * nf] * amp_ref[t:t + 1, cut]
        out_ref[:, cut] = total


def split3(v):
    hi = v.astype(bf16).astype(f32)
    rest = v - hi
    mid = rest.astype(bf16).astype(f32)
    return hi, mid, rest - mid


def inverse_factor(a, o_ref, m_ref, t_ref, tb_ref, q_ref, hook=None, hook_at=0):
    n = a.shape[0]
    sub, lane, lane2 = iota((PANEL, n), 0), iota((PANEL, n), 1), iota((n, n), 1)
    zero = jnp.zeros((PANEL, n), f32)
    m_ref[...] = a
    tb_ref[...] = jnp.zeros((n, n), bf16)
    q_ref[...] = jnp.zeros((n, n), bf16)

    def body(b, rows):
        if hook is not None:
            pl.when(b == hook_at)(hook)
        off = pl.multiple_of(b * PANEL, PANEL)
        prev = off - PANEL
        cols = [
            jnp.take_along_axis(rows, jnp.zeros((PANEL, n), jnp.int32) + (off + l), axis=1)
            for l in range(PANEL)
        ]
        update = jnp.dot(tb_ref[...], q_ref[...], preferred_element_type=f32)
        hi, mid, low = split3(rows)
        turned = jnp.concatenate([rows, hi, hi, mid, hi, low, mid, zero], axis=0).T
        t_ref[...] = turned
        m_ref[...] = jnp.where((lane2 >= prev) & (lane2 < off), 0.0, m_ref[...]) - update
        tb_ref[...] = turned.astype(bf16)
        nxt = pl.multiple_of(jnp.minimum(off + PANEL, n - PANEL), PANEL)
        after = m_ref[pl.ds(nxt, PANEL), :]
        near = t_ref[pl.ds(nxt, PANEL), :]
        coup = [jnp.broadcast_to(near[:, l:l + 1], (PANEL, n)) for l in range(PANEL)]
        inside = (lane >= off) & (lane < off + PANEL)
        x = jnp.where(lane - off == sub, 1.0, jnp.where(inside, 0.0, rows))
        outs = invs = x
        for j in range(PANEL):
            pick = lambda v: jnp.broadcast_to(v[j:j + 1, :], (PANEL, n))
            inv = 1.0 / pick(cols[j])
            xj = pick(x)
            invs = jnp.where(sub == j, inv, invs)
            outs = jnp.where(sub == j, x, outs)
            mult = jnp.where(sub == j, 0.0, cols[j] * inv)
            for l in range(j + 1, PANEL):
                cols[l] = cols[l] - mult * pick(cols[l])
            x = x - mult * xj
        x = x * invs
        o_ref[pl.ds(off, PANEL), :] = jnp.where(lane - off <= sub, outs * jnp.sqrt(invs), 0.0)
        hi, mid, low = split3(x)
        q_ref[...] = jnp.concatenate([zero, hi, mid, hi, low, hi, mid, zero], axis=0).astype(bf16)
        terms = [coup[l] * jnp.broadcast_to(x[l:l + 1, :], (PANEL, n)) for l in range(PANEL)]
        while len(terms) > 1:
            terms = [terms[i] + terms[i + 1] for i in range(0, len(terms), 2)]
        return jnp.where(inside, 0.0, after) - terms[0]

    lax.fori_loop(0, n // PANEL, body, m_ref[0:PANEL, :])


def pieces(v):
    hi = v.astype(bf16)
    rest = v - hi.astype(f32)
    mid = rest.astype(bf16)
    return hi, mid, (rest - mid.astype(f32)).astype(bf16)


def product(a, b, axis):
    ah, am, al = pieces(a)
    bh, bm, bl = pieces(b)
    left, right = jnp.concatenate([ah, am], axis=1), jnp.concatenate([ah, al], axis=1)
    deep = lambda u, v: jnp.concatenate([u, v], axis=axis)
    mul = lambda u, v: lax.dot_general(u, v, (((1,), (axis,)), ((), ())), preferred_element_type=f32)
    n = b.shape[1 - axis]
    small = mul(right, deep(bl, bh))
    if n == 128:
        both = mul(left, jnp.concatenate([deep(bh, bh), deep(bm, bm)], axis=1 - axis))
        return both[:, :n] + (both[:, n:] + small)
    return mul(left, deep(bh, bh)) + (mul(left, deep(bm, bm)) + small)


def dot(a, b):
    return product(a, b, 0)


def dot_nt(a, b):
    return product(a, b, 1)


def split2(v):
    hi = v.astype(bf16)
    return jnp.concatenate([hi, (v - hi.astype(f32)).astype(bf16)], axis=0)


def tri(t, s):
    return t * (t + 1) // 2 + s


def tree_kernel(pattern_ref, amp_ref, table_any, fields_any, prior_ref, out_ref,
                table_ref, fields_ref, load_sem, accw_ref, acc_ref, cpart_ref, bt_ref, wall_ref, cpiece_ref, csum_ref, g_ref, linv_ref, x_ref, xt_ref, yt_ref, z_ref, m_ref, t_ref, tb_ref, q_ref,
                s4, s4r, c4, c4r, s3, s3r, c3, c3r, s2, s2r, c2, c2r, s1, s1r, c1, c1r, send_sem, recv_sem):
    tiers, patterns, knots = table_ref.shape
    nf = fields_ref.shape[0]
    top = tiers - 1
    region, obs = lax.axis_index("region"), lax.axis_index("obs")
    n_obs = 4
    quarter = nf // n_obs
    own = {4: s4, 3: s3, 2: s2, 1: s1}
    got = {4: s4r, 3: s3r, 2: s2r, 1: s1r}
    cown = {4: c4, 3: c3, 2: c2, 1: c1}
    cgot = {4: c4r, 3: c3r, 2: c2r, 1: c1r}
    y_peers = [(region, lax.rem(obs + d, n_obs)) for d in (2, 1, 3)]

    def flip(*bits):
        other = region
        for bit in bits:
            other = other + bit - 2 * bit * lax.rem(lax.div(region, bit), 2)
        return other, obs

    tree_peer = {4: flip(1), 3: flip(2), 2: flip(2, 4)}
    z_peers = [flip(16), flip(8), flip(8, 16)]
    started = []

    def make(src, dst, k, dev):
        copy = pltpu.make_async_remote_copy(
            src_ref=src, dst_ref=dst, send_sem=send_sem.at[k], recv_sem=recv_sem.at[k],
            device_id=dev, device_id_type=pl.DeviceIdType.MESH)
        started.append(copy)
        return copy

    def send(src, dst, k, dev):
        copy = make(src, dst, k, dev)
        copy.start()
        return copy

    barrier = pltpu.get_barrier_semaphore()
    peers = y_peers + list(tree_peer.values()) + z_peers
    for dev in peers:
        pl.semaphore_signal(barrier, inc=1, device_id=dev, device_id_type=pl.DeviceIdType.MESH)
    loads = [pltpu.make_async_copy(fields_any, fields_ref, load_sem.at[0]),
             pltpu.make_async_copy(table_any, table_ref, load_sem.at[1])]
    for load in loads:
        load.start()

    def amplitude_rows(cut):
        prod = amplitude_products(amp_ref[:, cut])
        hi = prod.astype(bf16)
        return jnp.concatenate([hi, (prod - hi.astype(f32)).astype(bf16)], axis=0)

    def field_rows(cut):
        amp = amp_ref[:, cut]
        fields = fields_ref[:, cut].astype(f32)
        return jnp.concatenate([(fields * amp[t:t + 1, :]).astype(bf16) for t in range(tiers)], axis=0)

    n_here = amp_ref.shape[1]
    fold = patterns // 2
    accumulate(pattern_ref, accw_ref, n_here, 8192, amplitude_rows, fold)
    wall_ref[obs, :, 0:fold] = accw_ref[0:16, :] + accw_ref[16:32, :]
    wall_ref[obs, :, fold:patterns] = accw_ref[32:48, :] + accw_ref[48:64, :]
    pl.semaphore_wait(barrier, len(peers))

    w_copies = [send(wall_ref.at[obs], wall_ref.at[obs], k, dev) for k, dev in enumerate(y_peers)]
    for load in loads:
        load.wait()
    accumulate(pattern_ref, acc_ref, n_here, 2048, field_rows)
    for t in range(tiers):
        v = split2(acc_ref[t * nf:(t + 1) * nf, :])
        both = jnp.dot(v, table_ref[t], preferred_element_type=f32)
        cpart_ref[t] = both[:nf] + both[nf:]
    rs_copies = [
        send(cpart_ref.at[:, pl.ds(pl.multiple_of(dev[1] * quarter, quarter), quarter), :], cpiece_ref.at[k], 3 + k, dev)
        for k, dev in enumerate(y_peers)
    ]
    for t in range(tiers):
        bt_ref[t] = table_ref[t].astype(f32).T.astype(bf16)
    for copy in w_copies:
        copy.wait_recv()
    w = (wall_ref[0] + wall_ref[1]) + (wall_ref[2] + wall_ref[3])

    def build(t, s):
        row = PAIR_ROW[(s, t)]
        scaled = bt_ref[t].astype(f32) * w[row:row + 1, :]
        both = lax.dot_general(split2(scaled), bt_ref[s], (((1,), (1,)), ((), ())), preferred_element_type=f32)
        g_ref[tri(t, s)] = both[:knots] + both[knots:]

    urgent = [(4, 4), (4, 3), (3, 3)]
    for t, s in urgent:
        build(t, s)
    eye = iota((knots, knots), 0) == iota((knots, knots), 1)
    core = lax.rem(region, 2)
    half = pl.ds(pl.multiple_of(core * (knots // 2), knots // 2), knots // 2)

    def factor(t, block, hook=None, hook_at=0):
        inverse_factor(block + jnp.where(eye, prior_ref[t:t + 1, :], 0.0), linv_ref.at[t],
                       m_ref, t_ref, tb_ref, q_ref, hook, hook_at)

    def first_block(t, g):
        last = t - 1
        xl = dot(linv_ref[t], g(t, last))
        x_ref[tri(last, last)] = xl
        xt_ref[tri(last, last)] = xl.T
        own[t][tri(last, last)] = g(last, last) - dot(xt_ref[tri(last, last)], xl)

    def other_blocks(t, g):
        last = t - 1
        rest = dot(linv_ref[t], jnp.concatenate([g(t, s) for s in range(last)], axis=1))
        for s in range(last):
            xs = rest[:, s * knots:(s + 1) * knots]
            x_ref[tri(last, s)] = xs
            xt_ref[tri(last, s)] = xs.T
        for u in range(last, -1, -1):
            width = min(u + 1, last)
            prod = dot(xt_ref[tri(last, u)], rest[:, :width * knots])
            for s in range(width):
                own[t][tri(u, s)] = g(u, s) - prod[:, s * knots:(s + 1) * knots]

    def projections(t, c):
        z = dot_nt(c(t), linv_ref[t])
        z_ref[t] = z
        red = dot(z, jnp.concatenate([x_ref[tri(t - 1, s)] for s in range(t)], axis=1))
        for s in range(t):
            cown[t][s] = c(s) - red[:, s * knots:(s + 1) * knots]

    def prepare_descent(t):
        y = dot(jnp.concatenate([xt_ref[tri(t - 1, s)] for s in range(t)], axis=0), linv_ref[t])
        for s in range(t):
            yt_ref[tri(t - 1, s)] = y[s * knots:(s + 1) * knots]
        z_ref[t] = dot(z_ref[t], linv_ref[t])

    def summed(t):
        return lambda u, s: own[t][tri(u, s)] + got[t][tri(u, s)]

    def csummed(t):
        return lambda s: cown[t][s] + cgot[t][s]

    g4 = lambda t, s: g_ref[tri(t, s)]
    sibling, across, beyond = tree_peer[4], tree_peer[3], tree_peer[2]

    factor(4, g4(4, 4))
    first_block(4, g4)
    a4 = send(s4.at[9], s4r.at[9], 9, sibling)
    for copy in rs_copies:
        copy.wait_recv()
    mine = pl.ds(pl.multiple_of(obs * quarter, quarter), quarter)
    csum_ref[:, mine, :] = cpart_ref[:, mine, :] + cpiece_ref[0] + cpiece_ref[1] + cpiece_ref[2]
    ag_copies = [
        send(csum_ref.at[:, mine, :], csum_ref.at[:, mine, :], 6 + k, dev) for k, dev in enumerate(y_peers)
    ]
    for t in range(top, -1, -1):
        for s in range(t, -1, -1):
            if (t, s) not in urgent:
                build(t, s)
    other_blocks(4, g4)
    b4 = send(s4.at[pl.ds(0, 9)], s4r.at[pl.ds(0, 9)], 10, sibling)
    a4.wait_recv()

    g3 = summed(4)
    factor(3, g3(3, 3))
    b4.wait_recv()
    first_block(3, g3)
    a3 = send(s3.at[5], s3r.at[5], 12, across)
    other_blocks(3, g3)
    near, far = pl.ds(2, 3), pl.ds(0, 2)
    b3 = send(s3.at[near, half, :], s3r.at[near, half, :], 13, across)
    d3 = send(s3.at[far, half, :], s3r.at[far, half, :], 14, across)
    for copy in ag_copies:
        copy.wait_recv()
    projections(4, lambda s: csum_ref[s])
    e4 = send(c4, c4r, 11, sibling)
    a3.wait_recv()

    g2 = summed(3)
    relay_near = make(s3r.at[near, half, :], s3r.at[near, half, :], 16, sibling)

    def hand_over():
        b3.wait_recv()
        relay_near.start()

    factor(2, g2(2, 2), hand_over, 5)
    relay_near.wait_recv()
    first_block(2, g2)
    a2 = send(s2.at[2], s2r.at[2], 18, beyond)
    d3.wait_recv()
    relay_far = send(s3r.at[far, half, :], s3r.at[far, half, :], 17, sibling)
    e4.wait_recv()
    projections(3, csummed(4))
    e3 = send(c3, c3r, 15, across)
    relay_far.wait_recv()
    other_blocks(2, g2)
    b2 = send(s2.at[pl.ds(0, 2)], s2r.at[pl.ds(0, 2)], 19, beyond)
    a2.wait_recv()

    g1 = summed(2)
    factor(1, g1(1, 1))
    b2.wait_recv()
    first_block(1, g1)
    a1 = [send(s1.at[0], s1r.at[k], 21 + k, dev) for k, dev in enumerate(z_peers)]
    e3.wait_recv()
    projections(2, csummed(3))
    e2 = send(c2, c2r, 20, beyond)
    prepare_descent(4)
    prepare_descent(3)
    e2.wait_recv()
    projections(1, csummed(2))
    e1 = [send(c1.at[0], c1r.at[k], 24 + k, dev) for k, dev in enumerate(z_peers)]
    prepare_descent(2)
    prepare_descent(1)
    for copy in a1:
        copy.wait_recv()
    factor(0, (s1[0] + s1r[1]) + (s1r[2] + s1r[0]))
    for copy in e1:
        copy.wait_recv()
    c0 = (c1[0] + c1r[1]) + (c1r[2] + c1r[0])
    wts = [dot(dot_nt(c0, linv_ref[0]), linv_ref[0])]
    left = {t: z_ref[t] for t in range(1, tiers)}
    for s in range(top):
        moved = dot(wts[s], jnp.concatenate([yt_ref[tri(t - 1, s)] for t in range(s + 1, tiers)], axis=1))
        for t in range(s + 1, tiers):
            left[t] = left[t] - moved[:, (t - s - 1) * knots:(t - s) * knots]
        wts.append(left[s + 1])
    for t in range(tiers):
        both = jnp.dot(split2(wts[t]), bt_ref[t], preferred_element_type=f32)
        out_ref[t * nf:(t + 1) * nf, :] = (both[:nf] + both[nf:]).astype(bf16)
    for copy in started:
        copy.wait_send()


def shards(pattern, amplitude, basis_table, fields, prior_precision):
    tiers, patterns, knots = basis_table.shape
    obs = pattern.shape[0]
    nf = fields.shape[0]
    pattern2 = pattern.reshape(obs // 128, 128)
    block = lambda n: pltpu.VMEM((n, knots, knots), f32)
    rhs = lambda n: pltpu.VMEM((n, nf, knots), f32)
    per_pattern = pl.pallas_call(
        tree_kernel,
        out_shape=jax.ShapeDtypeStruct((tiers * nf, patterns), bf16),
        in_specs=[
            pl.BlockSpec(memory_space=pltpu.VMEM), pl.BlockSpec(memory_space=pltpu.VMEM),
            pl.BlockSpec(memory_space=pl.ANY), pl.BlockSpec(memory_space=pl.ANY),
            pl.BlockSpec(memory_space=pltpu.VMEM),
        ],
        scratch_shapes=[
            pltpu.VMEM(basis_table.shape, bf16), pltpu.VMEM(fields.shape, bf16), pltpu.SemaphoreType.DMA((2,)),
            pltpu.VMEM((64, patterns // 2), f32), pltpu.VMEM((tiers * nf, patterns), f32), rhs(tiers),
            pltpu.VMEM((tiers, knots, patterns), bf16),
            pltpu.VMEM((4, 16, patterns), f32),
            pltpu.VMEM((3, tiers, nf // 4, knots), f32),
            rhs(tiers), block(15), block(5), block(10), block(10), block(10), rhs(5),
            pltpu.VMEM((knots, knots), f32), pltpu.VMEM((knots, knots), f32),
            pltpu.VMEM((knots, knots), bf16), pltpu.VMEM((knots, knots), bf16),
            block(10), block(10), rhs(4), rhs(4),
            block(6), block(6), rhs(3), rhs(3),
            block(3), block(3), rhs(2), rhs(2),
            block(1), block(3), rhs(1), rhs(3),
            pltpu.SemaphoreType.DMA((27,)), pltpu.SemaphoreType.DMA((27,)),
        ],
        compiler_params=pltpu.CompilerParams(collective_id=0, has_side_effects=True),
    )(pattern2, amplitude, basis_table, fields, prior_precision)
    chunk = min(2048, obs)
    return pl.pallas_call(
        fit_kernel,
        grid=(obs // chunk,),
        in_specs=[
            pl.BlockSpec((chunk // 128, 128), lambda i: (i, 0)),
            pl.BlockSpec((tiers, chunk), lambda i: (0, i)),
            pl.BlockSpec((tiers * nf, patterns), lambda i: (0, 0)),
        ],
        out_specs=pl.BlockSpec((nf, chunk), lambda i: (0, i)),
        out_shape=jax.ShapeDtypeStruct((nf, obs), f32),
    )(pattern2, amplitude, per_pattern)


def solution(mesh):
    return jax.shard_map(
        shards,
        mesh=mesh,
        in_specs=(
            P(("region", "obs")),
            P(None, ("region", "obs")),
            P(),
            P(None, ("region", "obs")),
            P(),
        ),
        out_specs=P(None, ("region", "obs")),
        check_vma=False,
    )
```

```python
import functools

import jax
import jax.numpy as jnp
from jax import lax
from jax.experimental import pallas as pl
from jax.experimental.pallas import tpu as pltpu
from jax.sharding import PartitionSpec as P

f32 = jnp.float32
bf16 = jnp.bfloat16
highest = lax.Precision.HIGHEST
PANEL = 16
PAIR_ROW = {(0, 3): 5, (1, 4): 6, (0, 4): 7, (0, 1): 8, (1, 2): 9, (2, 3): 10, (3, 4): 11,
            (0, 2): 12, (1, 3): 13, (2, 4): 14, (0, 0): 0, (1, 1): 1, (2, 2): 2, (3, 3): 3, (4, 4): 4}


def iota(shape, axis):
    return lax.broadcasted_iota(jnp.int32, shape, axis)


def amplitude_products(amp):
    n = amp.shape[1]
    a8 = jnp.concatenate([amp, jnp.zeros((3, n), f32)], axis=0)
    sub = iota((8, n), 0)
    up = lambda s: pltpu.roll(a8, s, 0)
    l0 = jnp.where(sub < 5, a8, jnp.where(sub < 7, up(5), up(7)))
    r0 = jnp.where(sub < 5, a8, jnp.where(sub < 7, up(2), up(3)))
    l1 = jnp.where(sub < 4, a8, jnp.where(sub < 7, up(4), 0.0))
    r1 = jnp.where(sub < 4, up(7), up(2))
    return jnp.concatenate([l0 * r0, l1 * r1], axis=0)


def one_hot(pattern_ref, first_row, rows, patterns, fold=None):
    parts, masks = [], []
    ids = iota((patterns, 128), 0)
    for r in range(rows):
        row = pattern_ref[pl.ds(first_row + r, 1), :]
        if fold is not None:
            below = row < fold
            masks.append(jnp.where(below, 1.0, 0.0))
            row = jnp.where(below, row, row - fold)
        parts.append((jnp.broadcast_to(row, (patterns, 128)) == ids).astype(f32).astype(bf16))
    hot = jnp.concatenate(parts, axis=1)
    return hot if fold is None else (hot, jnp.concatenate(masks, axis=1))


def accumulate(pattern_ref, acc_ref, obs, chunk, lhs_of, fold=None):
    patterns = acc_ref.shape[1]
    acc_ref[...] = jnp.zeros_like(acc_ref)

    def step(i, carry):
        lhs = lhs_of(pl.ds(pl.multiple_of(i * chunk, chunk), chunk))
        hot = one_hot(pattern_ref, i * (chunk // 128), chunk // 128, patterns, fold)
        if fold is not None:
            hot, below = hot
            first = lhs * below.astype(bf16)
            lhs = jnp.concatenate([first, lhs - first], axis=0)
        acc_ref[...] += lax.dot_general(lhs, hot, (((1,), (1,)), ((), ())), preferred_element_type=f32)
        return carry

    lax.fori_loop(0, obs // chunk, step, 0)


def fit_kernel(pattern_ref, amp_ref, f_ref, out_ref):
    tiers = amp_ref.shape[0]
    nf, chunk = out_ref.shape
    part_of = min(1024, chunk)
    for first in range(0, chunk, part_of):
        cut = slice(first, first + part_of)
        hot = one_hot(pattern_ref, first // 128, part_of // 128, f_ref.shape[1])
        part = jnp.dot(f_ref[...], hot, preferred_element_type=f32)
        total = part[:nf] * amp_ref[0:1, cut]
        for t in range(1, tiers):
            total = total + part[t * nf:(t + 1) * nf] * amp_ref[t:t + 1, cut]
        out_ref[:, cut] = total


def split3(v):
    hi = v.astype(bf16).astype(f32)
    rest = v - hi
    mid = rest.astype(bf16).astype(f32)
    return hi, mid, rest - mid


def inverse_factor(a, o_ref, m_ref, t_ref, tb_ref, q_ref, hook=None, hook_at=0):
    n = a.shape[0]
    sub, lane, lane2 = iota((PANEL, n), 0), iota((PANEL, n), 1), iota((n, n), 1)
    zero = jnp.zeros((PANEL, n), f32)
    m_ref[...] = a
    tb_ref[...] = jnp.zeros((n, n), bf16)
    q_ref[...] = jnp.zeros((n, n), bf16)

    def body(b, rows):
        if hook is not None:
            pl.when(b == hook_at)(hook)
        off = pl.multiple_of(b * PANEL, PANEL)
        prev = off - PANEL
        cols = [
            jnp.take_along_axis(rows, jnp.zeros((PANEL, n), jnp.int32) + (off + l), axis=1)
            for l in range(PANEL)
        ]
        update = jnp.dot(tb_ref[...], q_ref[...], preferred_element_type=f32)
        hi, mid, low = split3(rows)
        turned = jnp.concatenate([rows, hi, hi, mid, hi, low, mid, zero], axis=0).T
        t_ref[...] = turned
        m_ref[...] = jnp.where((lane2 >= prev) & (lane2 < off), 0.0, m_ref[...]) - update
        tb_ref[...] = turned.astype(bf16)
        nxt = pl.multiple_of(jnp.minimum(off + PANEL, n - PANEL), PANEL)
        after = m_ref[pl.ds(nxt, PANEL), :]
        near = t_ref[pl.ds(nxt, PANEL), :]
        coup = [jnp.broadcast_to(near[:, l:l + 1], (PANEL, n)) for l in range(PANEL)]
        inside = (lane >= off) & (lane < off + PANEL)
        x = jnp.where(lane - off == sub, 1.0, jnp.where(inside, 0.0, rows))
        outs = invs = x
        for j in range(PANEL):
            pick = lambda v: jnp.broadcast_to(v[j:j + 1, :], (PANEL, n))
            inv = 1.0 / pick(cols[j])
            xj = pick(x)
            invs = jnp.where(sub == j, inv, invs)
            outs = jnp.where(sub == j, x, outs)
            mult = jnp.where(sub == j, 0.0, cols[j] * inv)
            for l in range(j + 1, PANEL):
                cols[l] = cols[l] - mult * pick(cols[l])
            x = x - mult * xj
        x = x * invs
        o_ref[pl.ds(off, PANEL), :] = jnp.where(lane - off <= sub, outs * jnp.sqrt(invs), 0.0)
        hi, mid, low = split3(x)
        q_ref[...] = jnp.concatenate([zero, hi, mid, hi, low, hi, mid, zero], axis=0).astype(bf16)
        terms = [coup[l] * jnp.broadcast_to(x[l:l + 1, :], (PANEL, n)) for l in range(PANEL)]
        while len(terms) > 1:
            terms = [terms[i] + terms[i + 1] for i in range(0, len(terms), 2)]
        return jnp.where(inside, 0.0, after) - terms[0]

    lax.fori_loop(0, n // PANEL, body, m_ref[0:PANEL, :])


def pieces(v):
    hi = v.astype(bf16)
    rest = v - hi.astype(f32)
    mid = rest.astype(bf16)
    return hi, mid, (rest - mid.astype(f32)).astype(bf16)


def product(a, b, axis):
    ah, am, al = pieces(a)
    bh, bm, bl = pieces(b)
    left, right = jnp.concatenate([ah, am], axis=1), jnp.concatenate([ah, al], axis=1)
    deep = lambda u, v: jnp.concatenate([u, v], axis=axis)
    mul = lambda u, v: lax.dot_general(u, v, (((1,), (axis,)), ((), ())), preferred_element_type=f32)
    n = b.shape[1 - axis]
    small = mul(right, deep(bl, bh))
    if n == 128:
        both = mul(left, jnp.concatenate([deep(bh, bh), deep(bm, bm)], axis=1 - axis))
        return both[:, :n] + (both[:, n:] + small)
    return mul(left, deep(bh, bh)) + (mul(left, deep(bm, bm)) + small)


def dot(a, b):
    return product(a, b, 0)


def dot_nt(a, b):
    return product(a, b, 1)


def split2(v):
    hi = v.astype(bf16)
    return jnp.concatenate([hi, (v - hi.astype(f32)).astype(bf16)], axis=0)


def tri(t, s):
    return t * (t + 1) // 2 + s


def tree_kernel(pattern_ref, amp_ref, table_any, fields_any, prior_ref, out_ref,
                table_ref, fields_ref, load_sem, accw_ref, acc_ref, cpart_ref, bt_ref, wall_ref, cpiece_ref, csum_ref, g_ref, linv_ref, x_ref, xt_ref, yt_ref, z_ref, m_ref, t_ref, tb_ref, q_ref,
                s4, s4r, c4, c4r, s3, s3r, c3, c3r, s2, s2r, c2, c2r, s1, s1r, c1, c1r, send_sem, recv_sem):
    tiers, patterns, knots = table_ref.shape
    nf = fields_ref.shape[0]
    top = tiers - 1
    region, obs = lax.axis_index("region"), lax.axis_index("obs")
    n_obs = 4
    quarter = nf // n_obs
    own = {4: s4, 3: s3, 2: s2, 1: s1}
    got = {4: s4r, 3: s3r, 2: s2r, 1: s1r}
    cown = {4: c4, 3: c3, 2: c2, 1: c1}
    cgot = {4: c4r, 3: c3r, 2: c2r, 1: c1r}
    y_peers = [(region, lax.rem(obs + d, n_obs)) for d in (2, 1, 3)]

    def flip(*bits):
        other = region
        for bit in bits:
            other = other + bit - 2 * bit * lax.rem(lax.div(region, bit), 2)
        return other, obs

    tree_peer = {4: flip(1), 3: flip(2), 2: flip(2, 4)}
    z_peers = [flip(16), flip(8), flip(8, 16)]
    started = []

    def make(src, dst, k, dev):
        copy = pltpu.make_async_remote_copy(
            src_ref=src, dst_ref=dst, send_sem=send_sem.at[k], recv_sem=recv_sem.at[k],
            device_id=dev, device_id_type=pl.DeviceIdType.MESH)
        started.append(copy)
        return copy

    def send(src, dst, k, dev):
        copy = make(src, dst, k, dev)
        copy.start()
        return copy

    barrier = pltpu.get_barrier_semaphore()
    peers = y_peers + list(tree_peer.values()) + z_peers
    for dev in peers:
        pl.semaphore_signal(barrier, inc=1, device_id=dev, device_id_type=pl.DeviceIdType.MESH)
    loads = [pltpu.make_async_copy(fields_any, fields_ref, load_sem.at[0]),
             pltpu.make_async_copy(table_any, table_ref, load_sem.at[1])]
    for load in loads:
        load.start()

    def amplitude_rows(cut):
        prod = amplitude_products(amp_ref[:, cut])
        hi = prod.astype(bf16)
        return jnp.concatenate([hi, (prod - hi.astype(f32)).astype(bf16)], axis=0)

    def field_rows(cut):
        amp = amp_ref[:, cut]
        fields = fields_ref[:, cut].astype(f32)
        return jnp.concatenate([(fields * amp[t:t + 1, :]).astype(bf16) for t in range(tiers)], axis=0)

    n_here = amp_ref.shape[1]
    fold = patterns // 2
    accumulate(pattern_ref, accw_ref, n_here, 8192, amplitude_rows, fold)
    wall_ref[obs, :, 0:fold] = accw_ref[0:16, :] + accw_ref[16:32, :]
    wall_ref[obs, :, fold:patterns] = accw_ref[32:48, :] + accw_ref[48:64, :]
    pl.semaphore_wait(barrier, len(peers))

    w_copies = [send(wall_ref.at[obs], wall_ref.at[obs], k, dev) for k, dev in enumerate(y_peers)]
    for load in loads:
        load.wait()
    accumulate(pattern_ref, acc_ref, n_here, 4096, field_rows)
    for t in range(tiers):
        v = split2(acc_ref[t * nf:(t + 1) * nf, :])
        both = jnp.dot(v, table_ref[t], preferred_element_type=f32)
        cpart_ref[t] = both[:nf] + both[nf:]
    rs_copies = [
        send(cpart_ref.at[:, pl.ds(pl.multiple_of(dev[1] * quarter, quarter), quarter), :], cpiece_ref.at[k], 3 + k, dev)
        for k, dev in enumerate(y_peers)
    ]
    for t in range(tiers):
        bt_ref[t] = table_ref[t].astype(f32).T.astype(bf16)
    for copy in w_copies:
        copy.wait_recv()
    w = (wall_ref[0] + wall_ref[1]) + (wall_ref[2] + wall_ref[3])

    def build(t, s):
        row = PAIR_ROW[(s, t)]
        scaled = bt_ref[t].astype(f32) * w[row:row + 1, :]
        both = lax.dot_general(split2(scaled), bt_ref[s], (((1,), (1,)), ((), ())), preferred_element_type=f32)
        g_ref[tri(t, s)] = both[:knots] + both[knots:]

    urgent = [(4, 4), (4, 3), (3, 3)]
    for t, s in urgent:
        build(t, s)
    eye = iota((knots, knots), 0) == iota((knots, knots), 1)
    core = lax.rem(region, 2)
    half = pl.ds(pl.multiple_of(core * (knots // 2), knots // 2), knots // 2)

    def factor(t, block, hook=None, hook_at=0):
        inverse_factor(block + jnp.where(eye, prior_ref[t:t + 1, :], 0.0), linv_ref.at[t],
                       m_ref, t_ref, tb_ref, q_ref, hook, hook_at)

    def first_block(t, g):
        last = t - 1
        xl = dot(linv_ref[t], g(t, last))
        x_ref[tri(last, last)] = xl
        xt_ref[tri(last, last)] = xl.T
        own[t][tri(last, last)] = g(last, last) - dot(xt_ref[tri(last, last)], xl)

    def other_blocks(t, g):
        last = t - 1
        rest = dot(linv_ref[t], jnp.concatenate([g(t, s) for s in range(last)], axis=1))
        for s in range(last):
            xs = rest[:, s * knots:(s + 1) * knots]
            x_ref[tri(last, s)] = xs
            xt_ref[tri(last, s)] = xs.T
        for u in range(last, -1, -1):
            width = min(u + 1, last)
            prod = dot(xt_ref[tri(last, u)], rest[:, :width * knots])
            for s in range(width):
                own[t][tri(u, s)] = g(u, s) - prod[:, s * knots:(s + 1) * knots]

    def projections(t, c):
        z = dot_nt(c(t), linv_ref[t])
        z_ref[t] = z
        red = dot(z, jnp.concatenate([x_ref[tri(t - 1, s)] for s in range(t)], axis=1))
        for s in range(t):
            cown[t][s] = c(s) - red[:, s * knots:(s + 1) * knots]

    def prepare_descent(t):
        y = dot(jnp.concatenate([xt_ref[tri(t - 1, s)] for s in range(t)], axis=0), linv_ref[t])
        for s in range(t):
            yt_ref[tri(t - 1, s)] = y[s * knots:(s + 1) * knots]
        z_ref[t] = dot(z_ref[t], linv_ref[t])

    def summed(t):
        return lambda u, s: own[t][tri(u, s)] + got[t][tri(u, s)]

    def csummed(t):
        return lambda s: cown[t][s] + cgot[t][s]

    g4 = lambda t, s: g_ref[tri(t, s)]
    sibling, across, beyond = tree_peer[4], tree_peer[3], tree_peer[2]

    factor(4, g4(4, 4))
    first_block(4, g4)
    a4 = send(s4.at[9], s4r.at[9], 9, sibling)
    for copy in rs_copies:
        copy.wait_recv()
    mine = pl.ds(pl.multiple_of(obs * quarter, quarter), quarter)
    csum_ref[:, mine, :] = cpart_ref[:, mine, :] + cpiece_ref[0] + cpiece_ref[1] + cpiece_ref[2]
    ag_copies = [
        send(csum_ref.at[:, mine, :], csum_ref.at[:, mine, :], 6 + k, dev) for k, dev in enumerate(y_peers)
    ]
    for t in range(top, -1, -1):
        for s in range(t, -1, -1):
            if (t, s) not in urgent:
                build(t, s)
    other_blocks(4, g4)
    b4 = send(s4.at[pl.ds(0, 9)], s4r.at[pl.ds(0, 9)], 10, sibling)
    a4.wait_recv()

    g3 = summed(4)
    factor(3, g3(3, 3))
    b4.wait_recv()
    first_block(3, g3)
    a3 = send(s3.at[5], s3r.at[5], 12, across)
    other_blocks(3, g3)
    near, far = pl.ds(2, 3), pl.ds(0, 2)
    b3 = send(s3.at[near, half, :], s3r.at[near, half, :], 13, across)
    d3 = send(s3.at[far, half, :], s3r.at[far, half, :], 14, across)
    for copy in ag_copies:
        copy.wait_recv()
    projections(4, lambda s: csum_ref[s])
    e4 = send(c4, c4r, 11, sibling)
    a3.wait_recv()

    g2 = summed(3)
    relay_near = make(s3r.at[near, half, :], s3r.at[near, half, :], 16, sibling)

    def hand_over():
        b3.wait_recv()
        relay_near.start()

    factor(2, g2(2, 2), hand_over, 5)
    relay_near.wait_recv()
    first_block(2, g2)
    a2 = send(s2.at[2], s2r.at[2], 18, beyond)
    d3.wait_recv()
    relay_far = send(s3r.at[far, half, :], s3r.at[far, half, :], 17, sibling)
    e4.wait_recv()
    projections(3, csummed(4))
    e3 = send(c3, c3r, 15, across)
    relay_far.wait_recv()
    other_blocks(2, g2)
    b2 = send(s2.at[pl.ds(0, 2)], s2r.at[pl.ds(0, 2)], 19, beyond)
    a2.wait_recv()

    g1 = summed(2)
    factor(1, g1(1, 1))
    b2.wait_recv()
    first_block(1, g1)
    a1 = [send(s1.at[0], s1r.at[k], 21 + k, dev) for k, dev in enumerate(z_peers)]
    e3.wait_recv()
    projections(2, csummed(3))
    e2 = send(c2, c2r, 20, beyond)
    prepare_descent(4)
    prepare_descent(3)
    e2.wait_recv()
    projections(1, csummed(2))
    e1 = [send(c1.at[0], c1r.at[k], 24 + k, dev) for k, dev in enumerate(z_peers)]
    prepare_descent(2)
    prepare_descent(1)
    for copy in a1:
        copy.wait_recv()
    factor(0, (s1[0] + s1r[1]) + (s1r[2] + s1r[0]))
    for copy in e1:
        copy.wait_recv()
    c0 = (c1[0] + c1r[1]) + (c1r[2] + c1r[0])
    wts = [dot(dot_nt(c0, linv_ref[0]), linv_ref[0])]
    left = {t: z_ref[t] for t in range(1, tiers)}
    for s in range(top):
        moved = dot(wts[s], jnp.concatenate([yt_ref[tri(t - 1, s)] for t in range(s + 1, tiers)], axis=1))
        for t in range(s + 1, tiers):
            left[t] = left[t] - moved[:, (t - s - 1) * knots:(t - s) * knots]
        wts.append(left[s + 1])
    for t in range(tiers):
        both = jnp.dot(split2(wts[t]), bt_ref[t], preferred_element_type=f32)
        out_ref[t * nf:(t + 1) * nf, :] = (both[:nf] + both[nf:]).astype(bf16)
    for copy in started:
        copy.wait_send()


def shards(pattern, amplitude, basis_table, fields, prior_precision):
    tiers, patterns, knots = basis_table.shape
    obs = pattern.shape[0]
    nf = fields.shape[0]
    pattern2 = pattern.reshape(obs // 128, 128)
    block = lambda n: pltpu.VMEM((n, knots, knots), f32)
    rhs = lambda n: pltpu.VMEM((n, nf, knots), f32)
    per_pattern = pl.pallas_call(
        tree_kernel,
        out_shape=jax.ShapeDtypeStruct((tiers * nf, patterns), bf16),
        in_specs=[
            pl.BlockSpec(memory_space=pltpu.VMEM), pl.BlockSpec(memory_space=pltpu.VMEM),
            pl.BlockSpec(memory_space=pl.ANY), pl.BlockSpec(memory_space=pl.ANY),
            pl.BlockSpec(memory_space=pltpu.VMEM),
        ],
        scratch_shapes=[
            pltpu.VMEM(basis_table.shape, bf16), pltpu.VMEM(fields.shape, bf16), pltpu.SemaphoreType.DMA((2,)),
            pltpu.VMEM((64, patterns // 2), f32), pltpu.VMEM((tiers * nf, patterns), f32), rhs(tiers),
            pltpu.VMEM((tiers, knots, patterns), bf16),
            pltpu.VMEM((4, 16, patterns), f32),
            pltpu.VMEM((3, tiers, nf // 4, knots), f32),
            rhs(tiers), block(15), block(5), block(10), block(10), block(10), rhs(5),
            pltpu.VMEM((knots, knots), f32), pltpu.VMEM((knots, knots), f32),
            pltpu.VMEM((knots, knots), bf16), pltpu.VMEM((knots, knots), bf16),
            block(10), block(10), rhs(4), rhs(4),
            block(6), block(6), rhs(3), rhs(3),
            block(3), block(3), rhs(2), rhs(2),
            block(1), block(3), rhs(1), rhs(3),
            pltpu.SemaphoreType.DMA((27,)), pltpu.SemaphoreType.DMA((27,)),
        ],
        compiler_params=pltpu.CompilerParams(collective_id=0, has_side_effects=True),
    )(pattern2, amplitude, basis_table, fields, prior_precision)
    chunk = min(4096, obs)
    return pl.pallas_call(
        fit_kernel,
        grid=(obs // chunk,),
        in_specs=[
            pl.BlockSpec((chunk // 128, 128), lambda i: (i, 0)),
            pl.BlockSpec((tiers, chunk), lambda i: (0, i)),
            pl.BlockSpec((tiers * nf, patterns), lambda i: (0, 0)),
        ],
        out_specs=pl.BlockSpec((nf, chunk), lambda i: (0, i)),
        out_shape=jax.ShapeDtypeStruct((nf, obs), f32),
    )(pattern2, amplitude, per_pattern)


def solution(mesh):
    return jax.shard_map(
        shards,
        mesh=mesh,
        in_specs=(
            P(("region", "obs")),
            P(None, ("region", "obs")),
            P(),
            P(None, ("region", "obs")),
            P(),
        ),
        out_specs=P(None, ("region", "obs")),
        check_vma=False,
    )
```
